32 devices in a mesh: grp: 2 (over y), patch: 4 (over z), lead: 4 (over x, core).
Axes of the slice: x: 2, y: 2, z: 4, core: 2. Of those that a mesh axis runs over, the one named last changes fastest.
Arguments:
- features: bfloat16 [8, 4, 128, 32, 128], P(('grp', 'lead'), 'patch'), parts along dimension 0, may hold values from -6 to 6
- context: bfloat16 [4, 8, 128, 2048], P('patch', ('grp', 'lead')), parts along dimension 1, may hold values from -6 to 6
- owner: int32 [8], P('grp'), parts along dimension 0, may hold values from 0 to 3, as said below
- hours: int32 [8], P('grp'), parts along dimension 0, may hold values from 0 to 18, as said below
- w_first: bfloat16 [9, 192, 128], replicated, may hold values from -0.15625 to 0.15625
- w_second: bfloat16 [9, 128, 128], replicated, may hold values from -0.1875 to 0.1875
- w_lead_in: bfloat16 [128, 32], replicated, may hold values from -0.5 to 0.5
- w_lead_mix: bfloat16 [3, 32, 32], replicated, may hold values from -0.625 to 0.625
- w_lead_out: bfloat16 [32, 128], replicated, may hold values from -1 to 1
Outputs:
- updated: bfloat16 [8, 4, 128, 32, 128], P(('grp', 'lead'), 'patch'), parts along dimension 0
The draws below stay inside these ranges and needn't reach their ends.
There are 2 independent parts, one for each index of `grp`. The reference program is written for one: setup_inputs(seed, part) draws one part's arguments, and reference() takes and returns one part's arrays. A program takes and returns all parts, laid end to end along the dimension named above; an argument that names none is the same for every part. Nothing has to cross between parts.
Inputs may be any that keep to these rules, and one draw needn't show every extreme that they name: `owner`: values are patch indices; some lead hour is owned by patch 0 and some by patch 4 - 1. `hours`: strictly increasing along the lead hours; consecutive differences run from 1 to 6, both reached; the last lead hour is the largest value.
All inputs are finite; a program needn't handle non-finite values.
Results may differ from the reference program's by a relative error of at most 0.0037.
Values may be sent and summed in bfloat16 or wider, within the bound.
A program may use at most 64 MiB of HBM per device.

```python
import jax
import jax.numpy as jnp
from jax import lax

H = 128
W = 32
CF = 128
CC = 64
CT = 32
LEADS = 4
PATCHES = 4


def draw_owner(key, part):
    picked = jax.random.randint(key, (LEADS,), 0, PATCHES)
    order = jax.random.permutation(jax.random.fold_in(key, 7), LEADS)
    picked = picked.at[order[0]].set(0)
    picked = picked.at[order[1]].set(PATCHES - 1)
    return picked.astype(jnp.int32)


def draw_hours(key, part):
    stride = jax.random.randint(key, (LEADS - 1,), 1, 7)
    order = jax.random.permutation(jax.random.fold_in(key, 11), LEADS - 1)
    stride = stride.at[order[0]].set(1)
    stride = stride.at[order[1]].set(6)
    rising = jnp.concatenate([jnp.zeros((1,), jnp.int32), jnp.cumsum(stride).astype(jnp.int32)])
    return (rising + 6 * (LEADS - 1) - rising[LEADS - 1]).astype(jnp.int32)


def block_scale(own_key, shape, cuts, least, high):
    loudness = 1.0
    for position, parts in cuts:
        draws = jax.random.uniform(jax.random.fold_in(jax.random.fold_in(own_key, 6), position), (parts,), jnp.float32, least / len(cuts), high / len(cuts))
        loudness = loudness * jnp.repeat(jnp.exp(draws), shape[position] // parts).reshape((-1,) + (1,) * (len(shape) - 1 - position))
    return loudness


def normal_values(stream_key, dims, scale, reach, pieces=(), held_as=jnp.bfloat16):
    values = scale * jax.random.normal(stream_key, dims, jnp.float32)
    if pieces:
        values = values * block_scale(stream_key, dims, pieces, -0.22, 0.18)
    return jnp.clip(values, -reach, reach).astype(held_as)


def setup_inputs(seed: int = 0, part: int = 0) -> dict:
    arg_keys = jax.random.split(jax.random.key(seed), 10)
    part_splits = jax.random.split(jax.random.fold_in(arg_keys[9], part), 10)
    features = normal_values(part_splits[0], (LEADS, PATCHES, H, W, CF), 1.0, 6.0, ((0, 4), (1, 4)))
    context = normal_values(part_splits[1], (PATCHES, LEADS, H, W * CC), 1.0, 6.0, ((0, 4), (1, 4)))
    owner = draw_owner(jax.random.fold_in(jax.random.fold_in(arg_keys[9], part), 71), part)
    hours = draw_hours(jax.random.fold_in(jax.random.fold_in(arg_keys[9], part), 71), part)
    w_first = normal_values(arg_keys[4], (9, CF + CC, CF), (9 * (CF + CC)) ** -0.5, 0.15625)
    w_second = normal_values(arg_keys[5], (9, CF, CF), (9 * CF) ** -0.5, 0.1875)
    w_lead_in = normal_values(arg_keys[6], (CF, CT), CF ** -0.5, 0.5)
    w_lead_mix = normal_values(arg_keys[7], (3, CT, CT), (3 * CT) ** -0.5, 0.625)
    w_lead_out = normal_values(arg_keys[8], (CT, CF), CT ** -0.5, 1.0)
    return dict(features=features, context=context, owner=owner, hours=hours, w_first=w_first, w_second=w_second, w_lead_in=w_lead_in, w_lead_mix=w_lead_mix, w_lead_out=w_lead_out)


def conv_padded(padded, kernel, height, width):
    depth = padded.shape[2]
    total = jnp.zeros((height * width, kernel.shape[2]), jnp.float32)
    for tap_index in range(9):
        row_off, col_off = divmod(tap_index, 3)
        window = padded[row_off:row_off + height, col_off:col_off + width].reshape(height * width, depth)
        total = total + jnp.dot(window, kernel[tap_index], preferred_element_type=jnp.float32)
    return total


def conv3x3(field, kernel):
    height, width = field.shape[0], field.shape[1]
    padded = jnp.pad(field, ((1, 1), (1, 1), (0, 0)))
    return conv_padded(padded, kernel, height, width)


def reference(features, context, owner, hours, w_first, w_second, w_lead_in, w_lead_mix, w_lead_out):
    lead_range = jnp.arange(LEADS, dtype=jnp.int32)
    chosen = context[owner, lead_range]
    lead_proj = jnp.dot(features.reshape(-1, CF), w_lead_in, preferred_element_type=jnp.float32).astype(jnp.bfloat16)
    lead_proj = lead_proj.reshape(LEADS, PATCHES, H * W, CT)
    lead_padded = jnp.pad(lead_proj, ((1, 1), (0, 0), (0, 0), (0, 0)))
    hour_float = hours.astype(jnp.float32)
    hour_gaps = hour_float[1:] - hour_float[:-1]
    gap_weight = jnp.exp(-0.5 * (hour_gaps - 1.0))
    zero_one = jnp.zeros((1,), jnp.float32)
    gain_prev = jnp.concatenate([zero_one, gap_weight])
    gain_next = jnp.concatenate([gap_weight, zero_one])

    def single(flat_index):
        lead_index = flat_index // PATCHES
        patch_index = flat_index % PATCHES
        resident = features[lead_index, patch_index]
        glob = chosen[lead_index].reshape(H, W, CC)
        joined = jnp.concatenate([resident, glob], axis=-1)
        first_pre = conv3x3(joined, w_first)
        first_act = jax.nn.silu(first_pre).astype(jnp.bfloat16).reshape(H, W, CF)
        second_pre = conv3x3(first_act, w_second)
        proj_prev = lead_padded[lead_index, patch_index]
        proj_self = lead_padded[lead_index + 1, patch_index]
        proj_next = lead_padded[lead_index + 2, patch_index]
        mixed = gain_prev[lead_index] * jnp.dot(proj_prev, w_lead_mix[0], preferred_element_type=jnp.float32)
        mixed = mixed + jnp.dot(proj_self, w_lead_mix[1], preferred_element_type=jnp.float32)
        mixed = mixed + gain_next[lead_index] * jnp.dot(proj_next, w_lead_mix[2], preferred_element_type=jnp.float32)
        mixed = mixed.astype(jnp.bfloat16)
        lifted = jnp.dot(mixed, w_lead_out, preferred_element_type=jnp.float32)
        result = resident.reshape(H * W, CF).astype(jnp.float32) + jax.nn.silu(second_pre + lifted)
        return result.astype(jnp.bfloat16).reshape(H, W, CF)

    updated = lax.map(single, jnp.arange(LEADS * PATCHES, dtype=jnp.int32))
    return updated.reshape(LEADS, PATCHES, H, W, CF)
```

```python
import functools

import jax
import jax.numpy as jnp
from jax import lax
from jax.experimental import pallas as pl
from jax.experimental.pallas import tpu as pltpu
from jax.sharding import PartitionSpec as P

MESH = pl.DeviceIdType.MESH
ROWS = 16
SLICE = 8
HALVES = 2
LAG = 9
ACT = 3
FIN = 5
F32 = jnp.float32
BF16 = jnp.bfloat16


def silu(v):
    return 0.5 * v * (1.0 + jnp.tanh(0.5 * v))


def dot(a, b):
    return jnp.dot(a, b, preferred_element_type=F32)


def kernel(
    n, leads, owner_hbm, hours_hbm, f_hbm, c_hbm, w1_hbm, w2_hbm, wi_hbm, wm_hbm, wo_hbm, o_ref,
    f_ref, c_ref, w1_ref, w2_ref, wi_ref, wm_ref, wo_ref,
    xs, ys, acc, big_g, gt, ct, wf, wc, ws, wd, wp, wx, proj, prev, foll, mixed,
    up_in, down_in, up_out, down_out, owner_ref, hours_ref, small_sem, in_sem,
    up_send, up_recv, down_send, down_recv, lead_send, lead_recv,
):
    height, width, ch = f_ref.shape
    chunks = height // ROWS
    slices = height // SLICE
    half = ROWS // 2
    cells = ROWS * width
    part = c_ref.shape[3]
    ctx_ch = HALVES * part // width
    pieces = HALVES * slices
    per = ch // ctx_ch
    groups = width // per
    temporal = wi_ref.shape[0]
    packs = ch // temporal
    packed_rows = height * width // packs

    def fetch(i):
        source, target = (
            (f_hbm, f_ref), (wi_hbm, wi_ref), (w1_hbm, w1_ref), (w2_hbm, w2_ref),
            (wm_hbm, wm_ref), (wo_hbm, wo_ref), (owner_hbm, owner_ref), (hours_hbm, hours_ref),
        )[i]
        return pltpu.make_async_copy(source, target, in_sem.at[i])

    def fetch_context(half):
        return pltpu.make_async_copy(
            c_hbm.at[:, :, half * part : (half + 1) * part], c_ref.at[:, half], small_sem.at[half]
        )

    z = lax.axis_index("patch")
    lead = lax.axis_index("lead")
    first, last = z == 0, z == n - 1
    lead_first, lead_last = lead == 0, lead == leads - 1

    barrier = pltpu.get_barrier_semaphore()


    for cond, axis, index in (
        (jnp.logical_not(first), "patch", z - 1),
        (jnp.logical_not(last), "patch", z + 1),
        (jnp.logical_not(lead_first), "lead", lead - 1),
        (jnp.logical_not(lead_last), "lead", lead + 1),
    ):
        @pl.when(cond)
        def _(axis=axis, index=index):
            pl.semaphore_signal(barrier, inc=1, device_id={axis: index}, device_id_type=MESH)

    neighbours = (
        4
        - first.astype(jnp.int32)
        - last.astype(jnp.int32)
        - lead_first.astype(jnp.int32)
        - lead_last.astype(jnp.int32)
    )
    for i in (6, 7, 0, 1):
        fetch(i).start()
    for half in range(HALVES):
        fetch_context(half).start()
    for i in range(2, 6):
        fetch(i).start()

    pl.semaphore_wait(barrier, neighbours)

    def up_copy(src, c, half):
        at = HALVES * c + half
        return pltpu.make_async_remote_copy(
            src_ref=src, dst_ref=up_in.at[c, half], send_sem=up_send.at[at],
            recv_sem=up_recv.at[at], device_id={"patch": z + 1}, device_id_type=MESH,
        )

    def down_copy(src, c, half):
        at = HALVES * c + half
        return pltpu.make_async_remote_copy(
            src_ref=src, dst_ref=down_in.at[c, half], send_sem=down_send.at[at],
            recv_sem=down_recv.at[at], device_id={"patch": z - 1}, device_id_type=MESH,
        )

    @pl.when(first)
    def _():
        @pl.loop(0, slices)
        def _(c):
            for half in range(HALVES):
                up_copy(c_hbm.at[c, :, half * part : (half + 1) * part], c, half).start()

    @pl.when(last)
    def _():
        @pl.loop(0, slices)
        def _(c):
            for half in range(HALVES):
                down_copy(c_hbm.at[c, :, half * part : (half + 1) * part], c, half).start()

    def project():
        fetch(0).wait()
        fetch(1).wait()
        wp[...] = jnp.zeros_like(wp)
        parts = []
        whole = f_ref[...].reshape(height // packs, packs, width, ch)
        for q in range(packs):
            wp[q * temporal : (q + 1) * temporal, q * ch : (q + 1) * ch] = wi_ref[...]
            parts.append(whole[:, q].reshape(packed_rows, ch))
        total = lax.dot_general(
            jnp.concatenate(parts, axis=1), wp[...], (((1,), (1,)), ((), ())),
            preferred_element_type=F32,
        )
        proj[...] = total.astype(BF16)

    def pack_weights(target, source):
        zero = jnp.zeros((ch, ch), BF16)
        for r in range(4):
            for b in range(3):
                at = (3 * r + b) * ch
                for q in range(2):
                    a = r - q
                    block = source[3 * a + b, :ch, :] if 0 <= a <= 2 else zero
                    target[at : at + ch, q * ch : (q + 1) * ch] = block

    def pack_context_weights():
        small = jnp.zeros((ctx_ch, ch), BF16)
        for a in range(3):
            taps = [w1_ref[3 * a + b, ch:, :] for b in range(3)]
            for i, pair in enumerate(
                ((taps[1], taps[0]), (taps[2], taps[1]), (taps[0], small), (small, taps[2]))
            ):
                at = a * 4 * ctx_ch + i * ctx_ch
                for q in range(2):
                    wc[at : at + ctx_ch, q * ch : (q + 1) * ch] = pair[q]

    def pack_lead_weights():
        wd[...] = jnp.zeros_like(wd)
        wx[...] = jnp.zeros_like(wx)
        for q in range(packs):
            at = slice(q * temporal, (q + 1) * temporal)
            for t in range(3):
                wd[t, at, at] = wm_ref[t]
            wx[at, q * ch : (q + 1) * ch] = wo_ref[...]

    def put_shifted(target, v, row, count):
        size = count * width
        col = lax.rem(lax.broadcasted_iota(jnp.int32, (size, ch), 0), width)
        left = jnp.where(col == 0, 0.0, pltpu.roll(v, 1, 0))
        right = jnp.where(col == width - 1, 0.0, pltpu.roll(v, size - 1, 0))
        for b, value in enumerate((left, v, right)):
            target[b, pl.ds(1 + row, count)] = value.astype(BF16).reshape(count, width, ch)

    def clear_edges():
        edge = jnp.zeros((width, ch), BF16)
        for target in (xs, ys):
            for b in range(3):
                target[b, 0] = edge
                target[b, height + 1] = edge
        big_g[0] = jnp.zeros(big_g.shape[1:], BF16)
        big_g[height + 1] = jnp.zeros(big_g.shape[1:], BF16)

    def shift_features():
        @pl.loop(0, chunks)
        def _(k):
            put_shifted(xs, f_ref[pl.ds(k * ROWS, ROWS)].reshape(cells, ch).astype(F32), k * ROWS, ROWS)

    def lead_copy(side):
        landing, index = ((prev, lead + 1), (foll, lead - 1))[side]
        return pltpu.make_async_remote_copy(
            src_ref=proj, dst_ref=landing, send_sem=lead_send.at[side],
            recv_sem=lead_recv.at[side], device_id={"lead": index}, device_id_type=MESH,
        )

    def send_projection():
        @pl.when(jnp.logical_not(lead_last))
        def _():
            lead_copy(0).start()

        @pl.when(jnp.logical_not(lead_first))
        def _():
            lead_copy(1).start()

    def conv_pairs(source, weights, row, count):
        pairs = count // 2
        parts = [
            source[b, pl.ds(row, count + 2)].reshape(pairs + 1, 2, width, ch) for b in range(3)
        ]
        lhs = [
            parts[b][r // 2 : r // 2 + pairs, r % 2].reshape(pairs * width, ch)
            for r in range(4)
            for b in range(3)
        ]
        return dot(jnp.concatenate(lhs, axis=1), weights[...])

    def split_pairs(out, count):
        return [
            out[:, q * ch : (q + 1) * ch].reshape(count // 2, width, ch) for q in range(2)
        ]

    def feature_conv(k):
        out = split_pairs(conv_pairs(xs, wf, k * ROWS, ROWS), ROWS)
        acc[pl.ds(k * ROWS, ROWS)] = jnp.stack(out, axis=1).reshape(ROWS, width, ch)

    def mix():
        @pl.when(jnp.logical_not(lead_first))
        def _():
            lead_copy(0).wait_recv()

        @pl.when(jnp.logical_not(lead_last))
        def _():
            lead_copy(1).wait_recv()

        @pl.when(lead_first)
        def _():
            prev[...] = jnp.zeros_like(prev)

        @pl.when(lead_last)
        def _():
            foll[...] = jnp.zeros_like(foll)

        now = hours_ref[lead]
        before = hours_ref[jnp.maximum(lead - 1, 0)]
        after = hours_ref[jnp.minimum(lead + 1, leads - 1)]

        def gain(later, earlier, absent):
            gap = jnp.full((1, ch), (later - earlier).astype(F32), F32)
            return jnp.where(absent, 0.0, jnp.exp(-0.5 * (gap - 1.0)))

        gain_prev = gain(now, before, lead_first)
        gain_next = gain(after, now, lead_last)
        value = gain_prev * dot(prev[...], wd[0])
        value = value + dot(proj[...], wd[1])
        value = value + gain_next * dot(foll[...], wd[2])
        mixed[...] = value.astype(BF16)

    total_rows = SLICE * groups

    def take_context(k):
        lane = lax.broadcasted_iota(jnp.int32, (total_rows, ch), 1)
        group = lax.rem(lax.broadcasted_iota(jnp.int32, (total_rows, ch), 0), groups)
        owner = owner_ref[lead]
        per_half = groups // HALVES
        for half in range(HALVES):
            low = jnp.where(owner < z, up_in[k, half], down_in[k, half])
            g = jnp.where(owner == z, c_ref[k, half], low).astype(F32)
            for j in range(per_half):
                at = half * per_half + j
                gt[pl.ds(at, SLICE, stride=groups), :] = g[:, j * ch : (j + 1) * ch]
        x = gt[...]
        y = pltpu.roll(x, ctx_ch, 1)
        back = jnp.where(group == 0, 0.0, pltpu.roll(y, 1, 0))
        ahead = jnp.where(group == groups - 1, 0.0, pltpu.roll(y, total_rows - 1, 0))
        beside = jnp.where(lane < ctx_ch, back, ahead)
        rows = pl.ds(1 + k * SLICE, SLICE)
        big_g[rows, :, :ch] = x.astype(BF16).reshape(SLICE, groups, ch)
        big_g[rows, :, ch:] = beside.astype(BF16).reshape(SLICE, groups, ch)

    def activate(row, count):
        size = count * groups
        lhs = [big_g[pl.ds(row + a, count)].reshape(size, 2 * ch) for a in range(3)]
        out = dot(jnp.concatenate(lhs, axis=1), wc[...])
        for q in range(2):
            ct[pl.ds(q, size, stride=2), :] = out[:, q * ch : (q + 1) * ch]
        v = silu(ct[: 2 * size] + acc[pl.ds(row, count)].reshape(2 * size, ch))
        put_shifted(ys, v, row, count)

    def finish(row, count):
        pairs, rows = count // 2, pl.ds(row, count)
        skip = row % packs if isinstance(row, int) else packs - 2
        out = split_pairs(conv_pairs(ys, ws, row, count), count)
        packed = (skip + count + packs - 1) // packs
        if isinstance(row, int):
            at = (row - skip) // packs * width
        else:
            at = pl.multiple_of(lax.div(row - skip, packs) * width, width)
        lift = dot(mixed[pl.ds(at, packed * width)], wx[...])
        lifted = [
            lift[i // packs * width : (i // packs + 1) * width, i % packs * ch : (i % packs + 1) * ch]
            for i in range(skip, skip + count)
        ]
        own = f_ref[rows].reshape(pairs, 2, width, ch)
        results = []
        for q in range(2):
            pre = out[q] + jnp.stack(lifted[q::2])
            results.append((own[:, q].astype(F32) + silu(pre)).astype(BF16))
        o_ref[rows] = jnp.stack(results, axis=1).reshape(count, width, ch)

    project()
    send_projection()
    shift_features()
    clear_edges()
    for half in range(HALVES):
        fetch_context(half).wait()
    fetch(6).wait()
    fetch(7).wait()

    def pack_first():
        fetch(2).wait()
        pack_weights(wf, w1_ref)
        pack_context_weights()

    def pack_rest():
        for i in (3, 4, 5):
            fetch(i).wait()
        pack_weights(ws, w2_ref)
        pack_lead_weights()

    def wait_piece(copy, landed, c):
        for half in range(HALVES):
            copy(landed.at[c, half], c, half).wait_recv()

    edge = first | last

    @pl.when(edge)
    def _():
        pack_first()

        @pl.loop(0, chunks)
        def _(k):
            feature_conv(k)

        pack_rest()
        mix()

        def receive(c):
            @pl.when(first)
            def _():
                wait_piece(down_copy, down_in, c)

            @pl.when(last)
            def _():
                wait_piece(up_copy, up_in, c)

            take_context(c)

        @pl.loop(0, slices)
        def _(c):
            receive(c)

            @pl.when(c == 1)
            def _():
                activate(0, ROWS - 1)
                finish(0, ROWS - 2)

            @pl.when((c > 1) & (c < slices - 2) & (lax.rem(c, 2) == 1))
            def _():
                row = lax.div(c, 2) * ROWS
                activate(row - 1, ROWS)
                finish(row - 2, ROWS)

            @pl.when(c == slices - 2)
            def _():
                activate(height - ROWS - 1, SLICE)
                finish(height - ROWS - 2, SLICE)

    @pl.when(jnp.logical_not(edge))
    def _():
        up_at, down_at = LAG * z, LAG * (n - 1 - z)
        ready_at = jnp.maximum(up_at, down_at)
        up_first = up_at >= down_at
        start_at = jnp.minimum(up_at, down_at)
        owner = owner_ref[lead]
        mine = owner == z

        def go(at, copy, landed, out):
            c, half = lax.div(at, HALVES), lax.rem(at, HALVES)

            @pl.when((at >= 0) & (at < pieces))
            def _():
                copy(landed.at[c, half], c, half).wait_recv()
                out[c, half] = jnp.where(mine, c_ref[c, half], landed[c, half])
                copy(out.at[c, half], c, half).start()

        @pl.loop(start_at, ready_at + pieces)
        def _(s):
            @pl.when(up_first)
            def _():
                go(s - up_at, up_copy, up_in, up_out)
                go(s - down_at, down_copy, down_in, down_out)

            @pl.when(jnp.logical_not(up_first))
            def _():
                go(s - down_at, down_copy, down_in, down_out)
                go(s - up_at, up_copy, up_in, up_out)

            t = s - start_at

            @pl.when(t <= chunks + 2)
            def _():
                @pl.when(t == 0)
                def _():
                    pack_first()

                @pl.when((t >= 1) & (t <= chunks))
                def _():
                    feature_conv(t - 1)

                @pl.when(t == chunks + 1)
                def _():
                    pack_rest()

                @pl.when(t == chunks + 2)
                def _():
                    mix()

            r = s - ready_at

            @pl.when(r >= 1)
            def _():
                @pl.when(lax.rem(r, 2) == 1)
                def _():
                    take_context(lax.div(r, 2))

                @pl.when(r == ACT)
                def _():
                    activate(0, ROWS - 1)

                @pl.when(r == FIN)
                def _():
                    finish(0, ROWS - 2)

                ra = r - ACT

                @pl.when((ra >= 4) & (ra < 4 * (chunks - 1)) & (lax.rem(ra, 4) == 0))
                def _():
                    activate(ra * (ROWS // 4) - 1, ROWS)

                rf = r - FIN

                @pl.when((rf >= 4) & (rf < 4 * (chunks - 1)) & (lax.rem(rf, 4) == 0))
                def _():
                    finish(rf * (ROWS // 4) - 2, ROWS)

        activate(height - ROWS - 1, SLICE)
        finish(height - ROWS - 2, SLICE)

    activate(height - SLICE - 1, SLICE + 1)
    finish(height - SLICE - 2, SLICE + 2)

    @pl.loop(0, slices)
    def _(c):
        for half in range(HALVES):
            @pl.when(jnp.logical_not(last))
            def _():
                up_copy(c_ref.at[c, half], c, half).wait_send()

            @pl.when(jnp.logical_not(first))
            def _():
                down_copy(c_ref.at[c, half], c, half).wait_send()

    @pl.when(jnp.logical_not(lead_last))
    def _():
        lead_copy(0).wait_send()

    @pl.when(jnp.logical_not(lead_first))
    def _():
        lead_copy(1).wait_send()


def per_device(
    features, context, owner, hours, w_first, w_second, w_lead_in, w_lead_mix, w_lead_out
):
    n, leads = lax.axis_size("patch"), lax.axis_size("lead")
    _, _, height, width, ch = features.shape
    temporal = w_lead_in.shape[1]
    merged = context.shape[3]
    cells = ROWS * width
    groups = merged // ch
    packs = ch // temporal
    packed_rows = height * width // packs
    vmem = pltpu.VMEM
    slices = height // SLICE
    pieces = HALVES * slices
    line = vmem((slices, HALVES, SLICE, merged // HALVES), BF16)
    hbm = pl.BlockSpec(memory_space=pl.ANY)
    dma = pltpu.SemaphoreType.DMA
    out = pl.pallas_call(
        functools.partial(kernel, n, leads),
        out_shape=vmem((height, width, ch), BF16),
        in_specs=[hbm] * 9,
        out_specs=pl.BlockSpec(memory_space=pltpu.VMEM),
        scratch_shapes=[
            vmem((height, width, ch), BF16),
            line,
            vmem(w_first.shape, BF16),
            vmem(w_second.shape, BF16),
            vmem((temporal, ch), BF16),
            vmem(w_lead_mix.shape, BF16),
            vmem(w_lead_out.shape, BF16),
            vmem((3, height + 2, width, ch), BF16),
            vmem((3, height + 2, width, ch), BF16),
            vmem((height, width, ch), F32),
            vmem((height + 2, groups, 2 * ch), BF16),
            vmem((SLICE * groups, ch), F32),
            vmem((cells, ch), F32),
            vmem((12 * ch, 2 * ch), BF16),
            vmem((6 * ch, 2 * ch), BF16),
            vmem((12 * ch, 2 * ch), BF16),
            vmem((3, ch, ch), BF16),
            vmem((ch, packs * ch), BF16),
            vmem((ch, packs * ch), BF16),
            vmem((packed_rows, ch), BF16),
            vmem((packed_rows, ch), BF16),
            vmem((packed_rows, ch), BF16),
            vmem((packed_rows, ch), BF16),
            line, line, line, line,
            pltpu.SMEM(owner.shape, jnp.int32), pltpu.SMEM(hours.shape, jnp.int32),
            dma((HALVES,)), dma((8,)),
            dma((pieces,)), dma((pieces,)), dma((pieces,)), dma((pieces,)), dma((2,)), dma((2,)),
        ],
        compiler_params=pltpu.CompilerParams(collective_id=0, has_side_effects=True),
    )(
        owner, hours, features[0, 0], context.reshape(slices, SLICE, merged),
        w_first, w_second, w_lead_in.T, w_lead_mix, w_lead_out,
    )
    return out[None, None]


def solution(mesh):
    placed = (
        P(("grp", "lead"), "patch", None, None, None),
        P("patch", ("grp", "lead"), None, None),
        P("grp"),
        P("grp"),
        P(),
        P(),
        P(),
        P(),
        P(),
    )
    return jax.shard_map(
        per_device,
        mesh=mesh,
        in_specs=placed,
        out_specs=P(("grp", "lead"), "patch", None, None, None),
        check_vma=False,
    )
```

```python
import functools

import jax
import jax.numpy as jnp
from jax import lax
from jax.experimental import pallas as pl
from jax.experimental.pallas import tpu as pltpu
from jax.sharding import PartitionSpec as P

MESH = pl.DeviceIdType.MESH
ROWS = 16
SLICE = 8
HALVES = 1
LAG = 5
EARLY = 2
F32 = jnp.float32
BF16 = jnp.bfloat16


def silu(v):
    return 0.5 * v * (1.0 + jnp.tanh(0.5 * v))


def dot(a, b):
    return jnp.dot(a, b, preferred_element_type=F32)


def kernel(
    n, leads, owner_hbm, hours_hbm, f_hbm, c_hbm, w1_hbm, w2_hbm, wi_hbm, wm_hbm, wo_hbm, o_ref,
    f_ref, c_ref, w1_ref, w2_ref, wi_ref, wm_ref, wo_ref,
    xs, ys, acc, big_g, gt, ct, wf, wc, ws, wd, wp, wx, proj, prev, foll, mixed,
    up_in, down_in, up_out, down_out, owner_ref, hours_ref, small_sem, in_sem,
    up_send, up_recv, down_send, down_recv, lead_send, lead_recv,
):
    height, width, ch = f_ref.shape
    chunks = height // ROWS
    slices = height // SLICE
    half = ROWS // 2
    cells = ROWS * width
    part = c_ref.shape[3]
    ctx_ch = HALVES * part // width
    pieces = HALVES * slices
    per = ch // ctx_ch
    groups = width // per
    temporal = wi_ref.shape[0]
    packs = ch // temporal
    packed_rows = height * width // packs

    def fetch(i):
        source, target = (
            (f_hbm, f_ref), (wi_hbm, wi_ref), (w1_hbm, w1_ref), (w2_hbm, w2_ref),
            (wm_hbm, wm_ref), (wo_hbm, wo_ref), (owner_hbm, owner_ref), (hours_hbm, hours_ref),
        )[i]
        return pltpu.make_async_copy(source, target, in_sem.at[i])

    def fetch_context(half):
        return pltpu.make_async_copy(
            c_hbm.at[:, :, half * part : (half + 1) * part], c_ref.at[:, half], small_sem.at[half]
        )

    z = lax.axis_index("patch")
    lead = lax.axis_index("lead")
    first, last = z == 0, z == n - 1
    lead_first, lead_last = lead == 0, lead == leads - 1

    barrier = pltpu.get_barrier_semaphore()


    for cond, axis, index in (
        (jnp.logical_not(first), "patch", z - 1),
        (jnp.logical_not(last), "patch", z + 1),
        (jnp.logical_not(lead_first), "lead", lead - 1),
        (jnp.logical_not(lead_last), "lead", lead + 1),
    ):
        @pl.when(cond)
        def _(axis=axis, index=index):
            pl.semaphore_signal(barrier, inc=1, device_id={axis: index}, device_id_type=MESH)

    neighbours = (
        4
        - first.astype(jnp.int32)
        - last.astype(jnp.int32)
        - lead_first.astype(jnp.int32)
        - lead_last.astype(jnp.int32)
    )
    for i in (6, 7, 0, 1):
        fetch(i).start()
    for half in range(HALVES):
        fetch_context(half).start()
    for i in range(2, 6):
        fetch(i).start()

    pl.semaphore_wait(barrier, neighbours)

    def up_copy(src, c, half):
        at = HALVES * c + half
        return pltpu.make_async_remote_copy(
            src_ref=src, dst_ref=up_in.at[c, half], send_sem=up_send.at[at],
            recv_sem=up_recv.at[at], device_id={"patch": z + 1}, device_id_type=MESH,
        )

    def down_copy(src, c, half):
        at = HALVES * c + half
        return pltpu.make_async_remote_copy(
            src_ref=src, dst_ref=down_in.at[c, half], send_sem=down_send.at[at],
            recv_sem=down_recv.at[at], device_id={"patch": z - 1}, device_id_type=MESH,
        )

    @pl.when(first)
    def _():
        @pl.loop(0, slices)
        def _(c):
            for half in range(HALVES):
                up_copy(c_hbm.at[c, :, half * part : (half + 1) * part], c, half).start()

    @pl.when(last)
    def _():
        @pl.loop(0, slices)
        def _(c):
            for half in range(HALVES):
                down_copy(c_hbm.at[c, :, half * part : (half + 1) * part], c, half).start()

    def project():
        fetch(0).wait()
        fetch(1).wait()
        wp[...] = jnp.zeros_like(wp)
        parts = []
        whole = f_ref[...].reshape(height // packs, packs, width, ch)
        for q in range(packs):
            wp[q * temporal : (q + 1) * temporal, q * ch : (q + 1) * ch] = wi_ref[...]
            parts.append(whole[:, q].reshape(packed_rows, ch))
        total = lax.dot_general(
            jnp.concatenate(parts, axis=1), wp[...], (((1,), (1,)), ((), ())),
            preferred_element_type=F32,
        )
        proj[...] = total.astype(BF16)

    def pack_weights(target, source):
        zero = jnp.zeros((ch, ch), BF16)
        for r in range(4):
            for b in range(3):
                at = (3 * r + b) * ch
                for q in range(2):
                    a = r - q
                    block = source[3 * a + b, :ch, :] if 0 <= a <= 2 else zero
                    target[at : at + ch, q * ch : (q + 1) * ch] = block

    def pack_context_weights():
        small = jnp.zeros((ctx_ch, ch), BF16)
        for a in range(3):
            taps = [w1_ref[3 * a + b, ch:, :] for b in range(3)]
            for i, pair in enumerate(
                ((taps[1], taps[0]), (taps[2], taps[1]), (taps[0], small), (small, taps[2]))
            ):
                at = a * 4 * ctx_ch + i * ctx_ch
                for q in range(2):
                    wc[at : at + ctx_ch, q * ch : (q + 1) * ch] = pair[q]

    def pack_lead_weights():
        wd[...] = jnp.zeros_like(wd)
        wx[...] = jnp.zeros_like(wx)
        for q in range(packs):
            at = slice(q * temporal, (q + 1) * temporal)
            for t in range(3):
                wd[t, at, at] = wm_ref[t]
            wx[at, q * ch : (q + 1) * ch] = wo_ref[...]

    def put_shifted(target, v, row, count):
        size = count * width
        col = lax.rem(lax.broadcasted_iota(jnp.int32, (size, ch), 0), width)
        left = jnp.where(col == 0, 0.0, pltpu.roll(v, 1, 0))
        right = jnp.where(col == width - 1, 0.0, pltpu.roll(v, size - 1, 0))
        for b, value in enumerate((left, v, right)):
            target[b, pl.ds(1 + row, count)] = value.astype(BF16).reshape(count, width, ch)

    def clear_edges():
        edge = jnp.zeros((width, ch), BF16)
        for target in (xs, ys):
            for b in range(3):
                target[b, 0] = edge
                target[b, height + 1] = edge
        big_g[0] = jnp.zeros(big_g.shape[1:], BF16)
        big_g[height + 1] = jnp.zeros(big_g.shape[1:], BF16)

    def shift_features():
        @pl.loop(0, chunks)
        def _(k):
            put_shifted(xs, f_ref[pl.ds(k * ROWS, ROWS)].reshape(cells, ch).astype(F32), k * ROWS, ROWS)

    def lead_copy(side):
        landing, index = ((prev, lead + 1), (foll, lead - 1))[side]
        return pltpu.make_async_remote_copy(
            src_ref=proj, dst_ref=landing, send_sem=lead_send.at[side],
            recv_sem=lead_recv.at[side], device_id={"lead": index}, device_id_type=MESH,
        )

    def send_projection():
        @pl.when(jnp.logical_not(lead_last))
        def _():
            lead_copy(0).start()

        @pl.when(jnp.logical_not(lead_first))
        def _():
            lead_copy(1).start()

    def conv_pairs(source, weights, row, count):
        pairs = count // 2
        parts = [
            source[b, pl.ds(row, count + 2)].reshape(pairs + 1, 2, width, ch) for b in range(3)
        ]
        lhs = [
            parts[b][r // 2 : r // 2 + pairs, r % 2].reshape(pairs * width, ch)
            for r in range(4)
            for b in range(3)
        ]
        return dot(jnp.concatenate(lhs, axis=1), weights[...])

    def split_pairs(out, count):
        return [
            out[:, q * ch : (q + 1) * ch].reshape(count // 2, width, ch) for q in range(2)
        ]

    def feature_conv(k):
        out = split_pairs(conv_pairs(xs, wf, k * ROWS, ROWS), ROWS)
        acc[pl.ds(k * ROWS, ROWS)] = jnp.stack(out, axis=1).reshape(ROWS, width, ch)

    def mix():
        @pl.when(jnp.logical_not(lead_first))
        def _():
            lead_copy(0).wait_recv()

        @pl.when(jnp.logical_not(lead_last))
        def _():
            lead_copy(1).wait_recv()

        @pl.when(lead_first)
        def _():
            prev[...] = jnp.zeros_like(prev)

        @pl.when(lead_last)
        def _():
            foll[...] = jnp.zeros_like(foll)

        now = hours_ref[lead]
        before = hours_ref[jnp.maximum(lead - 1, 0)]
        after = hours_ref[jnp.minimum(lead + 1, leads - 1)]

        def gain(later, earlier, absent):
            gap = jnp.full((1, ch), (later - earlier).astype(F32), F32)
            return jnp.where(absent, 0.0, jnp.exp(-0.5 * (gap - 1.0)))

        gain_prev = gain(now, before, lead_first)
        gain_next = gain(after, now, lead_last)
        value = gain_prev * dot(prev[...], wd[0])
        value = value + dot(proj[...], wd[1])
        value = value + gain_next * dot(foll[...], wd[2])
        mixed[...] = value.astype(BF16)

    total_rows = SLICE * groups

    def take_context(k):
        lane = lax.broadcasted_iota(jnp.int32, (total_rows, ch), 1)
        group = lax.rem(lax.broadcasted_iota(jnp.int32, (total_rows, ch), 0), groups)
        owner = owner_ref[lead]
        per_half = groups // HALVES
        for half in range(HALVES):
            low = jnp.where(owner < z, up_in[k, half], down_in[k, half])
            g = jnp.where(owner == z, c_ref[k, half], low).astype(F32)
            for j in range(per_half):
                at = half * per_half + j
                gt[pl.ds(at, SLICE, stride=groups), :] = g[:, j * ch : (j + 1) * ch]
        x = gt[...]
        y = pltpu.roll(x, ctx_ch, 1)
        back = jnp.where(group == 0, 0.0, pltpu.roll(y, 1, 0))
        ahead = jnp.where(group == groups - 1, 0.0, pltpu.roll(y, total_rows - 1, 0))
        beside = jnp.where(lane < ctx_ch, back, ahead)
        rows = pl.ds(1 + k * SLICE, SLICE)
        big_g[rows, :, :ch] = x.astype(BF16).reshape(SLICE, groups, ch)
        big_g[rows, :, ch:] = beside.astype(BF16).reshape(SLICE, groups, ch)

    def activate(row, count):
        size = count * groups
        lhs = [big_g[pl.ds(row + a, count)].reshape(size, 2 * ch) for a in range(3)]
        out = dot(jnp.concatenate(lhs, axis=1), wc[...])
        for q in range(2):
            ct[pl.ds(q, size, stride=2), :] = out[:, q * ch : (q + 1) * ch]
        v = silu(ct[: 2 * size] + acc[pl.ds(row, count)].reshape(2 * size, ch))
        put_shifted(ys, v, row, count)

    def finish(row, count):
        pairs, rows = count // 2, pl.ds(row, count)
        skip = row % packs if isinstance(row, int) else packs - 2
        out = split_pairs(conv_pairs(ys, ws, row, count), count)
        packed = (skip + count + packs - 1) // packs
        if isinstance(row, int):
            at = (row - skip) // packs * width
        else:
            at = pl.multiple_of(lax.div(row - skip, packs) * width, width)
        lift = dot(mixed[pl.ds(at, packed * width)], wx[...])
        lifted = [
            lift[i // packs * width : (i // packs + 1) * width, i % packs * ch : (i % packs + 1) * ch]
            for i in range(skip, skip + count)
        ]
        own = f_ref[rows].reshape(pairs, 2, width, ch)
        results = []
        for q in range(2):
            pre = out[q] + jnp.stack(lifted[q::2])
            results.append((own[:, q].astype(F32) + silu(pre)).astype(BF16))
        o_ref[rows] = jnp.stack(results, axis=1).reshape(count, width, ch)

    project()
    send_projection()
    shift_features()
    clear_edges()
    fetch(2).wait()
    pack_weights(wf, w1_ref)
    pack_context_weights()

    @pl.loop(0, EARLY)
    def _(k):
        feature_conv(k)

    for half in range(HALVES):
        fetch_context(half).wait()
    fetch(6).wait()
    fetch(7).wait()

    def pack_rest():
        for i in (3, 4, 5):
            fetch(i).wait()
        pack_weights(ws, w2_ref)
        pack_lead_weights()

    def wait_piece(copy, landed, c):
        for half in range(HALVES):
            copy(landed.at[c, half], c, half).wait_recv()

    edge = first | last

    @pl.when(edge)
    def _():
        @pl.loop(EARLY, chunks)
        def _(k):
            feature_conv(k)

        pack_rest()
        mix()

        def receive(c):
            @pl.when(first)
            def _():
                wait_piece(down_copy, down_in, c)

            @pl.when(last)
            def _():
                wait_piece(up_copy, up_in, c)

            take_context(c)

        @pl.loop(0, slices)
        def _(c):
            receive(c)

            @pl.when(c == 1)
            def _():
                activate(0, ROWS - 1)
                finish(0, ROWS - 2)

            @pl.when((c > 1) & (c < slices - 2) & (lax.rem(c, 2) == 1))
            def _():
                row = lax.div(c, 2) * ROWS
                activate(row - 1, ROWS)
                finish(row - 2, ROWS)

            @pl.when(c == slices - 2)
            def _():
                activate(height - ROWS - 1, SLICE)
                finish(height - ROWS - 2, SLICE)

    @pl.when(jnp.logical_not(edge))
    def _():
        up_at, down_at = LAG * z, LAG * (n - 1 - z)
        ready_at = jnp.maximum(up_at, down_at)
        up_first = up_at >= down_at
        start_at = jnp.minimum(up_at, down_at)
        owner = owner_ref[lead]
        mine = owner == z

        def go(at, copy, landed, out):
            c, half = lax.div(at, HALVES), lax.rem(at, HALVES)

            @pl.when((at >= 0) & (at < pieces))
            def _():
                copy(landed.at[c, half], c, half).wait_recv()
                out[c, half] = jnp.where(mine, c_ref[c, half], landed[c, half])
                copy(out.at[c, half], c, half).start()

        @pl.loop(start_at, ready_at + pieces)
        def _(s):
            @pl.when(up_first)
            def _():
                go(s - up_at, up_copy, up_in, up_out)
                go(s - down_at, down_copy, down_in, down_out)

            @pl.when(jnp.logical_not(up_first))
            def _():
                go(s - down_at, down_copy, down_in, down_out)
                go(s - up_at, up_copy, up_in, up_out)

            t = s - start_at

            @pl.when(t <= chunks - EARLY + 1)
            def _():
                @pl.when(t < chunks - EARLY)
                def _():
                    feature_conv(t + EARLY)

                @pl.when(t == chunks - EARLY)
                def _():
                    pack_rest()

                @pl.when(t == chunks - EARLY + 1)
                def _():
                    mix()

            r = s - ready_at

            @pl.when(r >= 0)
            def _():
                take_context(r)

                @pl.when(r == 1)
                def _():
                    activate(0, ROWS - 1)

                @pl.when(r == 2)
                def _():
                    finish(0, ROWS - 2)

                odd = lax.rem(r, 2)
                row = (r - odd) * SLICE

                @pl.when((r > 2) & (r < slices - 2) & (odd == 1))
                def _():
                    activate(row - 1, ROWS)

                @pl.when((r > 2) & (odd == 0))
                def _():
                    finish(row - ROWS - 2, ROWS)

        activate(height - ROWS - 1, SLICE)
        finish(height - ROWS - 2, SLICE)

    activate(height - SLICE - 1, SLICE + 1)
    finish(height - SLICE - 2, SLICE + 2)

    @pl.loop(0, slices)
    def _(c):
        for half in range(HALVES):
            @pl.when(jnp.logical_not(last))
            def _():
                up_copy(c_ref.at[c, half], c, half).wait_send()

            @pl.when(jnp.logical_not(first))
            def _():
                down_copy(c_ref.at[c, half], c, half).wait_send()

    @pl.when(jnp.logical_not(lead_last))
    def _():
        lead_copy(0).wait_send()

    @pl.when(jnp.logical_not(lead_first))
    def _():
        lead_copy(1).wait_send()


def per_device(
    features, context, owner, hours, w_first, w_second, w_lead_in, w_lead_mix, w_lead_out
):
    n, leads = lax.axis_size("patch"), lax.axis_size("lead")
    _, _, height, width, ch = features.shape
    temporal = w_lead_in.shape[1]
    merged = context.shape[3]
    cells = ROWS * width
    groups = merged // ch
    packs = ch // temporal
    packed_rows = height * width // packs
    vmem = pltpu.VMEM
    slices = height // SLICE
    pieces = HALVES * slices
    line = vmem((slices, HALVES, SLICE, merged // HALVES), BF16)
    hbm = pl.BlockSpec(memory_space=pl.ANY)
    dma = pltpu.SemaphoreType.DMA
    out = pl.pallas_call(
        functools.partial(kernel, n, leads),
        out_shape=vmem((height, width, ch), BF16),
        in_specs=[hbm] * 9,
        out_specs=pl.BlockSpec(memory_space=pltpu.VMEM),
        scratch_shapes=[
            vmem((height, width, ch), BF16),
            line,
            vmem(w_first.shape, BF16),
            vmem(w_second.shape, BF16),
            vmem((temporal, ch), BF16),
            vmem(w_lead_mix.shape, BF16),
            vmem(w_lead_out.shape, BF16),
            vmem((3, height + 2, width, ch), BF16),
            vmem((3, height + 2, width, ch), BF16),
            vmem((height, width, ch), F32),
            vmem((height + 2, groups, 2 * ch), BF16),
            vmem((SLICE * groups, ch), F32),
            vmem((cells, ch), F32),
            vmem((12 * ch, 2 * ch), BF16),
            vmem((6 * ch, 2 * ch), BF16),
            vmem((12 * ch, 2 * ch), BF16),
            vmem((3, ch, ch), BF16),
            vmem((ch, packs * ch), BF16),
            vmem((ch, packs * ch), BF16),
            vmem((packed_rows, ch), BF16),
            vmem((packed_rows, ch), BF16),
            vmem((packed_rows, ch), BF16),
            vmem((packed_rows, ch), BF16),
            line, line, line, line,
            pltpu.SMEM(owner.shape, jnp.int32), pltpu.SMEM(hours.shape, jnp.int32),
            dma((HALVES,)), dma((8,)),
            dma((pieces,)), dma((pieces,)), dma((pieces,)), dma((pieces,)), dma((2,)), dma((2,)),
        ],
        compiler_params=pltpu.CompilerParams(collective_id=0, has_side_effects=True),
    )(
        owner, hours, features[0, 0], context.reshape(slices, SLICE, merged),
        w_first, w_second, w_lead_in.T, w_lead_mix, w_lead_out,
    )
    return out[None, None]


def solution(mesh):
    placed = (
        P(("grp", "lead"), "patch", None, None, None),
        P("patch", ("grp", "lead"), None, None),
        P("grp"),
        P("grp"),
        P(),
        P(),
        P(),
        P(),
        P(),
    )
    return jax.shard_map(
        per_device,
        mesh=mesh,
        in_specs=placed,
        out_specs=P(("grp", "lead"), "patch", None, None, None),
        check_vma=False,
    )
```

```python
import functools

import jax
import jax.numpy as jnp
from jax import lax
from jax.experimental import pallas as pl
from jax.experimental.pallas import tpu as pltpu
from jax.sharding import PartitionSpec as P

MESH = pl.DeviceIdType.MESH
ROWS = 16
SLICE = 8
HALVES = 1
LAG = 5
LATE = 5
EARLY = 2
F32 = jnp.float32
BF16 = jnp.bfloat16


def silu(v):
    return 0.5 * v * (1.0 + jnp.tanh(0.5 * v))


def dot(a, b):
    return jnp.dot(a, b, preferred_element_type=F32)


def kernel(
    n, leads, owner_hbm, hours_hbm, f_hbm, c_hbm, w1_hbm, w2_hbm, wi_hbm, wm_hbm, wo_hbm, o_ref,
    f_ref, c_ref, w1_ref, w2_ref, wi_ref, wm_ref, wo_ref,
    xs, ys, acc, big_g, gt, wf, wc, ws, wd, wp, proj, prev, foll, mixed,
    up_in, down_in, up_out, down_out, owner_ref, hours_ref, small_sem, in_sem,
    up_send, up_recv, down_send, down_recv, lead_send, lead_recv,
):
    height, width, ch = f_ref.shape
    chunks = height // ROWS
    slices = height // SLICE
    half = ROWS // 2
    cells = ROWS * width
    part = c_ref.shape[3]
    ctx_ch = HALVES * part // width
    pieces = HALVES * slices
    per = ch // ctx_ch
    groups = width // per
    temporal = wi_ref.shape[0]
    packs = ch // temporal
    packed_rows = height * width // packs

    def fetch(i):
        source, target = (
            (f_hbm, f_ref), (wi_hbm, wi_ref), (w1_hbm, w1_ref), (w2_hbm, w2_ref),
            (wm_hbm, wm_ref), (wo_hbm, wo_ref), (owner_hbm, owner_ref), (hours_hbm, hours_ref),
        )[i]
        return pltpu.make_async_copy(source, target, in_sem.at[i])

    def fetch_context(half):
        return pltpu.make_async_copy(
            c_hbm.at[:, :, half * part : (half + 1) * part], c_ref.at[:, half], small_sem.at[half]
        )

    z = lax.axis_index("patch")
    lead = lax.axis_index("lead")
    first, last = z == 0, z == n - 1
    lead_first, lead_last = lead == 0, lead == leads - 1

    barrier = pltpu.get_barrier_semaphore()


    for cond, axis, index in (
        (jnp.logical_not(first), "patch", z - 1),
        (jnp.logical_not(last), "patch", z + 1),
        (jnp.logical_not(lead_first), "lead", lead - 1),
        (jnp.logical_not(lead_last), "lead", lead + 1),
    ):
        @pl.when(cond)
        def _(axis=axis, index=index):
            pl.semaphore_signal(barrier, inc=1, device_id={axis: index}, device_id_type=MESH)

    neighbours = (
        4
        - first.astype(jnp.int32)
        - last.astype(jnp.int32)
        - lead_first.astype(jnp.int32)
        - lead_last.astype(jnp.int32)
    )
    for i in (6, 7, 0, 1):
        fetch(i).start()
    for half in range(HALVES):
        fetch_context(half).start()
    for i in range(2, 6):
        fetch(i).start()

    pl.semaphore_wait(barrier, neighbours)

    def up_copy(src, c, half):
        at = HALVES * c + half
        return pltpu.make_async_remote_copy(
            src_ref=src, dst_ref=up_in.at[c, half], send_sem=up_send.at[at],
            recv_sem=up_recv.at[at], device_id={"patch": z + 1}, device_id_type=MESH,
        )

    def down_copy(src, c, half):
        at = HALVES * c + half
        return pltpu.make_async_remote_copy(
            src_ref=src, dst_ref=down_in.at[c, half], send_sem=down_send.at[at],
            recv_sem=down_recv.at[at], device_id={"patch": z - 1}, device_id_type=MESH,
        )

    @pl.when(first)
    def _():
        @pl.loop(0, slices)
        def _(c):
            for half in range(HALVES):
                up_copy(c_hbm.at[c, :, half * part : (half + 1) * part], c, half).start()

    @pl.when(last)
    def _():
        @pl.loop(0, slices)
        def _(c):
            for half in range(HALVES):
                down_copy(c_hbm.at[c, :, half * part : (half + 1) * part], c, half).start()

    def project():
        fetch(0).wait()
        fetch(1).wait()
        wp[...] = jnp.zeros_like(wp)
        parts = []
        whole = f_ref[...].reshape(height // packs, packs, width, ch)
        for q in range(packs):
            wp[q * temporal : (q + 1) * temporal, q * ch : (q + 1) * ch] = wi_ref[...]
            parts.append(whole[:, q].reshape(packed_rows, ch))
        total = lax.dot_general(
            jnp.concatenate(parts, axis=1), wp[...], (((1,), (1,)), ((), ())),
            preferred_element_type=F32,
        )
        proj[...] = total.astype(BF16)

    def pack_weights(target, source):
        zero = jnp.zeros((ch, ch), BF16)
        for r in range(4):
            for b in range(3):
                at = (3 * r + b) * ch
                for q in range(2):
                    a = r - q
                    block = source[3 * a + b, :ch, :] if 0 <= a <= 2 else zero
                    target[at : at + ch, q * ch : (q + 1) * ch] = block

    def pack_context_weights():
        small = jnp.zeros((ctx_ch, ch), BF16)
        for a in range(3):
            taps = [w1_ref[3 * a + b, ch:, :] for b in range(3)]
            for i, pair in enumerate(
                ((taps[1], taps[0]), (taps[2], taps[1]), (taps[0], small), (small, taps[2]))
            ):
                at = a * 4 * ctx_ch + i * ctx_ch
                for q in range(2):
                    wc[at : at + ctx_ch, q * ch : (q + 1) * ch] = pair[q]

    def pack_lead_weights():
        wd[...] = jnp.zeros_like(wd)
        ws[12 * ch :] = jnp.zeros((packs // 2 * ch, 2 * ch), BF16)
        for q in range(packs):
            at = slice(q * temporal, (q + 1) * temporal)
            for t in range(3):
                wd[t, at, at] = wm_ref[t]
            low = (12 + q // 2) * ch + q * temporal
            ws[low : low + temporal, q % 2 * ch : (q % 2 + 1) * ch] = wo_ref[...]

    def put_shifted(target, v, row, count):
        size = count * width
        col = lax.rem(lax.broadcasted_iota(jnp.int32, (size, ch), 0), width)
        left = jnp.where(col == 0, 0.0, pltpu.roll(v, 1, 0))
        right = jnp.where(col == width - 1, 0.0, pltpu.roll(v, size - 1, 0))
        for b, value in enumerate((left, v, right)):
            target[b, pl.ds(1 + row, count)] = value.astype(BF16).reshape(count, width, ch)

    def clear_edges():
        edge = jnp.zeros((width, ch), BF16)
        for target in (xs, ys):
            for b in range(3):
                target[b, 0] = edge
                target[b, height + 1] = edge
        big_g[0] = jnp.zeros(big_g.shape[1:], BF16)
        big_g[height + 1] = jnp.zeros(big_g.shape[1:], BF16)

    def shift_features():
        @pl.loop(0, chunks)
        def _(k):
            put_shifted(xs, f_ref[pl.ds(k * ROWS, ROWS)].reshape(cells, ch).astype(F32), k * ROWS, ROWS)

    def lead_copy(side):
        landing, index = ((prev, lead + 1), (foll, lead - 1))[side]
        return pltpu.make_async_remote_copy(
            src_ref=proj, dst_ref=landing, send_sem=lead_send.at[side],
            recv_sem=lead_recv.at[side], device_id={"lead": index}, device_id_type=MESH,
        )

    def send_projection():
        @pl.when(jnp.logical_not(lead_last))
        def _():
            lead_copy(0).start()

        @pl.when(jnp.logical_not(lead_first))
        def _():
            lead_copy(1).start()

    def conv_pairs(source, weights, row, count, more=()):
        pairs = count // 2
        parts = [
            source[b, pl.ds(row, count + 2)].reshape(pairs + 1, 2, width, ch) for b in range(3)
        ]
        lhs = [
            parts[b][r // 2 : r // 2 + pairs, r % 2].reshape(pairs * width, ch)
            for r in range(4)
            for b in range(3)
        ]
        return dot(jnp.concatenate(lhs + list(more), axis=1), weights[...])

    def split_pairs(out, count):
        return [
            out[:, q * ch : (q + 1) * ch].reshape(count // 2, width, ch) for q in range(2)
        ]

    def feature_conv(k):
        out = split_pairs(conv_pairs(xs, wf, k * ROWS, ROWS), ROWS)
        acc[pl.ds(k * ROWS, ROWS)] = jnp.stack(out, axis=1).reshape(ROWS, width, ch)

    def mix():
        @pl.when(jnp.logical_not(lead_first))
        def _():
            lead_copy(0).wait_recv()

        @pl.when(jnp.logical_not(lead_last))
        def _():
            lead_copy(1).wait_recv()

        @pl.when(lead_first)
        def _():
            prev[...] = jnp.zeros_like(prev)

        @pl.when(lead_last)
        def _():
            foll[...] = jnp.zeros_like(foll)

        now = hours_ref[lead]
        before = hours_ref[jnp.maximum(lead - 1, 0)]
        after = hours_ref[jnp.minimum(lead + 1, leads - 1)]

        def gain(later, earlier, absent):
            gap = jnp.full((1, ch), (later - earlier).astype(F32), F32)
            return jnp.where(absent, 0.0, jnp.exp(-0.5 * (gap - 1.0)))

        gain_prev = gain(now, before, lead_first)
        gain_next = gain(after, now, lead_last)
        value = gain_prev * dot(prev[...], wd[0])
        value = value + dot(proj[...], wd[1])
        value = value + gain_next * dot(foll[...], wd[2])
        mixed[...] = value.astype(BF16)

    total_rows = SLICE * groups

    def take_context(k):
        lane = lax.broadcasted_iota(jnp.int32, (total_rows, ch), 1)
        group = lax.rem(lax.broadcasted_iota(jnp.int32, (total_rows, ch), 0), groups)
        owner = owner_ref[lead]
        per_half = groups // HALVES
        for half in range(HALVES):
            low = jnp.where(owner < z, up_in[k, half], down_in[k, half])
            g = jnp.where(owner == z, c_ref[k, half], low).astype(F32)
            for j in range(per_half):
                at = half * per_half + j
                gt[pl.ds(at, SLICE, stride=groups), :] = g[:, j * ch : (j + 1) * ch]
        x = gt[...]
        y = pltpu.roll(x, ctx_ch, 1)
        back = jnp.where(group == 0, 0.0, pltpu.roll(y, 1, 0))
        ahead = jnp.where(group == groups - 1, 0.0, pltpu.roll(y, total_rows - 1, 0))
        beside = jnp.where(lane < ctx_ch, back, ahead)
        rows = pl.ds(1 + k * SLICE, SLICE)
        big_g[rows, :, :ch] = x.astype(BF16).reshape(SLICE, groups, ch)
        big_g[rows, :, ch:] = beside.astype(BF16).reshape(SLICE, groups, ch)

    def activate(row, count):
        size = count * groups
        lhs = [big_g[pl.ds(row + a, count)].reshape(size, 2 * ch) for a in range(3)]
        out = dot(jnp.concatenate(lhs, axis=1), wc[...])
        v = silu(out.reshape(2 * size, ch) + acc[pl.ds(row, count)].reshape(2 * size, ch))
        put_shifted(ys, v, row, count)

    def finish(row, count):
        pairs, rows = count // 2, pl.ds(row, count)
        skip = row % packs if isinstance(row, int) else packs - 2
        skip = row % packs if isinstance(row, int) else packs - 2
        packed = (skip + count + packs - 1) // packs
        if isinstance(row, int):
            at = (row - skip) // packs * width
        else:
            at = pl.multiple_of(lax.div(row - skip, packs) * width, width)
        near = mixed[pl.ds(at, packed * width)]
        none = jnp.zeros((width, ch), BF16)
        more = []
        for turn in range(packs // 2):
            blocks = []
            for i in range(skip, skip + count, 2):
                m = i // packs
                hit = i % packs // 2 == turn
                blocks.append(near[m * width : (m + 1) * width] if hit else none)
            more.append(jnp.concatenate(blocks, axis=0))
        out = split_pairs(conv_pairs(ys, ws, row, count, more), count)
        own = f_ref[rows].reshape(pairs, 2, width, ch)
        results = []
        for q in range(2):
            results.append((own[:, q].astype(F32) + silu(out[q])).astype(BF16))
        o_ref[rows] = jnp.stack(results, axis=1).reshape(count, width, ch)

    project()
    send_projection()
    shift_features()
    clear_edges()
    fetch(2).wait()
    pack_weights(wf, w1_ref)
    pack_context_weights()

    @pl.loop(0, EARLY)
    def _(k):
        feature_conv(k)

    for half in range(HALVES):
        fetch_context(half).wait()
    fetch(6).wait()
    fetch(7).wait()

    def pack_rest():
        for i in (3, 4, 5):
            fetch(i).wait()
        pack_weights(ws, w2_ref)
        pack_lead_weights()

    def wait_piece(copy, landed, c):
        for half in range(HALVES):
            copy(landed.at[c, half], c, half).wait_recv()

    edge = first | last

    @pl.when(edge)
    def _():
        @pl.loop(EARLY, chunks)
        def _(k):
            feature_conv(k)

        pack_rest()
        mix()

        def receive(c):
            @pl.when(first)
            def _():
                wait_piece(down_copy, down_in, c)

            @pl.when(last)
            def _():
                wait_piece(up_copy, up_in, c)

            take_context(c)

        @pl.loop(0, slices)
        def _(c):
            receive(c)

            @pl.when(c == 1)
            def _():
                activate(0, ROWS - 1)
                finish(0, ROWS - 2)

            @pl.when((c > 1) & (c < slices - 2) & (lax.rem(c, 2) == 1))
            def _():
                row = lax.div(c, 2) * ROWS
                activate(row - 1, ROWS)
                finish(row - 2, ROWS)


    @pl.when(jnp.logical_not(edge))
    def _():
        up_at, down_at = LAG * z, LAG * (n - 1 - z)
        ready_at = jnp.maximum(up_at, down_at)
        up_first = up_at >= down_at
        start_at = jnp.minimum(up_at, down_at)
        owner = owner_ref[lead]
        mine = owner == z

        def go(at, copy, landed, out):
            c, half = lax.div(at, HALVES), lax.rem(at, HALVES)

            @pl.when((at >= 0) & (at < pieces))
            def _():
                copy(landed.at[c, half], c, half).wait_recv()
                out[c, half] = jnp.where(mine, c_ref[c, half], landed[c, half])
                copy(out.at[c, half], c, half).start()

        @pl.loop(start_at, ready_at + pieces + LATE)
        def _(s):
            @pl.when(up_first)
            def _():
                go(s - up_at, up_copy, up_in, up_out)
                go(s - down_at, down_copy, down_in, down_out)

            @pl.when(jnp.logical_not(up_first))
            def _():
                go(s - down_at, down_copy, down_in, down_out)
                go(s - up_at, up_copy, up_in, up_out)

            t = s - start_at

            @pl.when(t <= chunks - EARLY + 1)
            def _():
                @pl.when(t < chunks - EARLY)
                def _():
                    feature_conv(t + EARLY)

                @pl.when(t == chunks - EARLY)
                def _():
                    pack_rest()

                @pl.when(t == chunks - EARLY + 1)
                def _():
                    mix()

            r = s - ready_at - LATE

            @pl.when(r >= 0)
            def _():
                take_context(r)

                @pl.when(r == 1)
                def _():
                    activate(0, ROWS - 1)

                @pl.when(r == 2)
                def _():
                    finish(0, ROWS - 2)

                odd = lax.rem(r, 2)
                row = (r - odd) * SLICE

                @pl.when((r > 2) & (r < slices - 2) & (odd == 1))
                def _():
                    activate(row - 1, ROWS)

                @pl.when((r > 2) & (odd == 0))
                def _():
                    finish(row - ROWS - 2, ROWS)

    activate(height - ROWS - 1, ROWS + 1)
    finish(height - ROWS - 2, ROWS + 2)

    @pl.loop(0, slices)
    def _(c):
        for half in range(HALVES):
            @pl.when(jnp.logical_not(last))
            def _():
                up_copy(c_ref.at[c, half], c, half).wait_send()

            @pl.when(jnp.logical_not(first))
            def _():
                down_copy(c_ref.at[c, half], c, half).wait_send()

    @pl.when(jnp.logical_not(lead_last))
    def _():
        lead_copy(0).wait_send()

    @pl.when(jnp.logical_not(lead_first))
    def _():
        lead_copy(1).wait_send()


def per_device(
    features, context, owner, hours, w_first, w_second, w_lead_in, w_lead_mix, w_lead_out
):
    n, leads = lax.axis_size("patch"), lax.axis_size("lead")
    _, _, height, width, ch = features.shape
    temporal = w_lead_in.shape[1]
    merged = context.shape[3]
    cells = ROWS * width
    groups = merged // ch
    packs = ch // temporal
    packed_rows = height * width // packs
    vmem = pltpu.VMEM
    slices = height // SLICE
    pieces = HALVES * slices
    line = vmem((slices, HALVES, SLICE, merged // HALVES), BF16)
    hbm = pl.BlockSpec(memory_space=pl.ANY)
    dma = pltpu.SemaphoreType.DMA
    out = pl.pallas_call(
        functools.partial(kernel, n, leads),
        out_shape=vmem((height, width, ch), BF16),
        in_specs=[hbm] * 9,
        out_specs=pl.BlockSpec(memory_space=pltpu.VMEM),
        scratch_shapes=[
            vmem((height, width, ch), BF16),
            line,
            vmem(w_first.shape, BF16),
            vmem(w_second.shape, BF16),
            vmem((temporal, ch), BF16),
            vmem(w_lead_mix.shape, BF16),
            vmem(w_lead_out.shape, BF16),
            vmem((3, height + 2, width, ch), BF16),
            vmem((3, height + 2, width, ch), BF16),
            vmem((height, width, ch), F32),
            vmem((height + 2, groups, 2 * ch), BF16),
            vmem((SLICE * groups, ch), F32),
            vmem((12 * ch, 2 * ch), BF16),
            vmem((6 * ch, 2 * ch), BF16),
            vmem(((12 + packs // 2) * ch, 2 * ch), BF16),
            vmem((3, ch, ch), BF16),
            vmem((ch, packs * ch), BF16),
            vmem((packed_rows, ch), BF16),
            vmem((packed_rows, ch), BF16),
            vmem((packed_rows, ch), BF16),
            vmem((packed_rows, ch), BF16),
            line, line, line, line,
            pltpu.SMEM(owner.shape, jnp.int32), pltpu.SMEM(hours.shape, jnp.int32),
            dma((HALVES,)), dma((8,)),
            dma((pieces,)), dma((pieces,)), dma((pieces,)), dma((pieces,)), dma((2,)), dma((2,)),
        ],
        compiler_params=pltpu.CompilerParams(collective_id=0, has_side_effects=True),
    )(
        owner, hours, features[0, 0], context.reshape(slices, SLICE, merged),
        w_first, w_second, w_lead_in.T, w_lead_mix, w_lead_out,
    )
    return out[None, None]


def solution(mesh):
    placed = (
        P(("grp", "lead"), "patch", None, None, None),
        P("patch", ("grp", "lead"), None, None),
        P("grp"),
        P("grp"),
        P(),
        P(),
        P(),
        P(),
        P(),
    )
    return jax.shard_map(
        per_device,
        mesh=mesh,
        in_specs=placed,
        out_specs=P(("grp", "lead"), "patch", None, None, None),
        check_vma=False,
    )
```

```python
import functools

import jax
import jax.numpy as jnp
from jax import lax
from jax.experimental import pallas as pl
from jax.experimental.pallas import tpu as pltpu
from jax.sharding import PartitionSpec as P

MESH = pl.DeviceIdType.MESH
ROWS = 16
SLICE = 8
HALVES = 1
LAG = 5
LIMIT = 56 * 2**20
LATE = 5
EARLY = 2
F32 = jnp.float32
BF16 = jnp.bfloat16


def silu(v):
    return 0.5 * v * (1.0 + jnp.tanh(0.5 * v))


def dot(a, b):
    return jnp.dot(a, b, preferred_element_type=F32)


def conv_pairs(source, weights, row, count, more=()):
    width, ch = source.shape[2:]
    pairs = count // 2
    parts = [
        source[b, pl.ds(row, count + 2)].reshape(pairs + 1, 2, width, ch) for b in range(3)
    ]
    lhs = [
        parts[b][r // 2 : r // 2 + pairs, r % 2].reshape(pairs * width, ch)
        for r in range(4)
        for b in range(3)
    ]
    return dot(jnp.concatenate(lhs + list(more), axis=1), weights[...])

def split_pairs(out, count, width):
    ch = out.shape[1] // 2
    return [
        out[:, q * ch : (q + 1) * ch].reshape(count // 2, width, ch) for q in range(2)
    ]


def finished(f_ref, ys, ws, mixed, row, count):
    height, width, ch = f_ref.shape
    packs = height * width // mixed.shape[0]
    pairs, rows = count // 2, pl.ds(row, count)
    skip = row % packs if isinstance(row, int) else packs - 2
    skip = row % packs if isinstance(row, int) else packs - 2
    packed = (skip + count + packs - 1) // packs
    if isinstance(row, int):
        at = (row - skip) // packs * width
    else:
        at = pl.multiple_of(lax.div(row - skip, packs) * width, width)
    near = mixed[pl.ds(at, packed * width)]
    none = jnp.zeros((width, ch), BF16)
    more = []
    for turn in range(packs // 2):
        blocks = []
        for i in range(skip, skip + count, 2):
            m = i // packs
            hit = i % packs // 2 == turn
            blocks.append(near[m * width : (m + 1) * width] if hit else none)
        more.append(jnp.concatenate(blocks, axis=0))
    out = split_pairs(conv_pairs(ys, ws, row, count, more), count, width)
    own = f_ref[rows].reshape(pairs, 2, width, ch)
    results = []
    for q in range(2):
        results.append((own[:, q].astype(F32) + silu(out[q])).astype(BF16))
    return jnp.stack(results, axis=1).reshape(count, width, ch)


def last_rows(o_in, f_ref, ys, ws, mixed, out_hbm, rest, sem):
    height = f_ref.shape[0]
    start = height - ROWS - 2
    early = pltpu.make_async_copy(o_in.at[:start], out_hbm.at[:start], sem.at[0])
    early.start()
    rest[...] = finished(f_ref, ys, ws, mixed, start, ROWS + 2)
    late = pltpu.make_async_copy(rest, out_hbm.at[start:], sem.at[1])
    late.start()
    early.wait()
    late.wait()


def kernel(
    n, leads, owner_hbm, hours_hbm, f_hbm, c_hbm, w1_hbm, w2_hbm, wi_hbm, wm_hbm, wo_hbm, o_ref, f_ref, ys, ws, mixed,
    c_ref, w1_ref, w2_ref, wi_ref, wm_ref, wo_ref,
    xs, acc, big_g, gt, wf, wc, wd, wp, proj, prev, foll,
    up_in, down_in, up_out, down_out, owner_ref, hours_ref, small_sem, in_sem,
    up_send, up_recv, down_send, down_recv, lead_send, lead_recv,
):
    height, width, ch = f_ref.shape
    chunks = height // ROWS
    slices = height // SLICE
    half = ROWS // 2
    cells = ROWS * width
    part = c_ref.shape[3]
    ctx_ch = HALVES * part // width
    pieces = HALVES * slices
    per = ch // ctx_ch
    groups = width // per
    temporal = wi_ref.shape[0]
    packs = ch // temporal
    packed_rows = height * width // packs

    def fetch(i):
        source, target = (
            (f_hbm, f_ref), (wi_hbm, wi_ref), (w1_hbm, w1_ref), (w2_hbm, w2_ref),
            (wm_hbm, wm_ref), (wo_hbm, wo_ref), (owner_hbm, owner_ref), (hours_hbm, hours_ref),
        )[i]
        return pltpu.make_async_copy(source, target, in_sem.at[i])

    def fetch_context(half):
        return pltpu.make_async_copy(
            c_hbm.at[:, :, half * part : (half + 1) * part], c_ref.at[:, half], small_sem.at[half]
        )

    z = lax.axis_index("patch")
    lead = lax.axis_index("lead")
    first, last = z == 0, z == n - 1
    lead_first, lead_last = lead == 0, lead == leads - 1

    barrier = pltpu.get_barrier_semaphore()


    for cond, axis, index in (
        (jnp.logical_not(first), "patch", z - 1),
        (jnp.logical_not(last), "patch", z + 1),
        (jnp.logical_not(lead_first), "lead", lead - 1),
        (jnp.logical_not(lead_last), "lead", lead + 1),
    ):
        @pl.when(cond)
        def _(axis=axis, index=index):
            pl.semaphore_signal(barrier, inc=1, device_id={axis: index}, device_id_type=MESH)

    neighbours = (
        4
        - first.astype(jnp.int32)
        - last.astype(jnp.int32)
        - lead_first.astype(jnp.int32)
        - lead_last.astype(jnp.int32)
    )
    for i in (6, 7, 0, 1):
        fetch(i).start()
    for half in range(HALVES):
        fetch_context(half).start()
    for i in range(2, 6):
        fetch(i).start()

    pl.semaphore_wait(barrier, neighbours)

    def up_copy(src, c, half):
        at = HALVES * c + half
        return pltpu.make_async_remote_copy(
            src_ref=src, dst_ref=up_in.at[c, half], send_sem=up_send.at[at],
            recv_sem=up_recv.at[at], device_id={"patch": z + 1}, device_id_type=MESH,
        )

    def down_copy(src, c, half):
        at = HALVES * c + half
        return pltpu.make_async_remote_copy(
            src_ref=src, dst_ref=down_in.at[c, half], send_sem=down_send.at[at],
            recv_sem=down_recv.at[at], device_id={"patch": z - 1}, device_id_type=MESH,
        )

    @pl.when(first)
    def _():
        @pl.loop(0, slices)
        def _(c):
            for half in range(HALVES):
                up_copy(c_hbm.at[c, :, half * part : (half + 1) * part], c, half).start()

    @pl.when(last)
    def _():
        @pl.loop(0, slices)
        def _(c):
            for half in range(HALVES):
                down_copy(c_hbm.at[c, :, half * part : (half + 1) * part], c, half).start()

    def project():
        fetch(0).wait()
        fetch(1).wait()
        wp[...] = jnp.zeros_like(wp)
        parts = []
        whole = f_ref[...].reshape(height // packs, packs, width, ch)
        for q in range(packs):
            wp[q * temporal : (q + 1) * temporal, q * ch : (q + 1) * ch] = wi_ref[...]
            parts.append(whole[:, q].reshape(packed_rows, ch))
        total = lax.dot_general(
            jnp.concatenate(parts, axis=1), wp[...], (((1,), (1,)), ((), ())),
            preferred_element_type=F32,
        )
        proj[...] = total.astype(BF16)

    def pack_weights(target, source):
        zero = jnp.zeros((ch, ch), BF16)
        for r in range(4):
            for b in range(3):
                at = (3 * r + b) * ch
                for q in range(2):
                    a = r - q
                    block = source[3 * a + b, :ch, :] if 0 <= a <= 2 else zero
                    target[at : at + ch, q * ch : (q + 1) * ch] = block

    def pack_context_weights():
        small = jnp.zeros((ctx_ch, ch), BF16)
        for a in range(3):
            taps = [w1_ref[3 * a + b, ch:, :] for b in range(3)]
            for i, pair in enumerate(
                ((taps[1], taps[0]), (taps[2], taps[1]), (taps[0], small), (small, taps[2]))
            ):
                at = a * 4 * ctx_ch + i * ctx_ch
                for q in range(2):
                    wc[at : at + ctx_ch, q * ch : (q + 1) * ch] = pair[q]

    def pack_lead_weights():
        wd[...] = jnp.zeros_like(wd)
        ws[12 * ch :] = jnp.zeros((packs // 2 * ch, 2 * ch), BF16)
        for q in range(packs):
            at = slice(q * temporal, (q + 1) * temporal)
            for t in range(3):
                wd[t, at, at] = wm_ref[t]
            low = (12 + q // 2) * ch + q * temporal
            ws[low : low + temporal, q % 2 * ch : (q % 2 + 1) * ch] = wo_ref[...]

    def put_shifted(target, v, row, count):
        size = count * width
        col = lax.rem(lax.broadcasted_iota(jnp.int32, (size, ch), 0), width)
        left = jnp.where(col == 0, 0.0, pltpu.roll(v, 1, 0))
        right = jnp.where(col == width - 1, 0.0, pltpu.roll(v, size - 1, 0))
        for b, value in enumerate((left, v, right)):
            target[b, pl.ds(1 + row, count)] = value.astype(BF16).reshape(count, width, ch)

    def clear_edges():
        edge = jnp.zeros((width, ch), BF16)
        for target in (xs, ys):
            for b in range(3):
                target[b, 0] = edge
                target[b, height + 1] = edge
        big_g[0] = jnp.zeros(big_g.shape[1:], BF16)
        big_g[height + 1] = jnp.zeros(big_g.shape[1:], BF16)

    def shift_features():
        @pl.loop(0, chunks)
        def _(k):
            put_shifted(xs, f_ref[pl.ds(k * ROWS, ROWS)].reshape(cells, ch).astype(F32), k * ROWS, ROWS)

    def lead_copy(side):
        landing, index = ((prev, lead + 1), (foll, lead - 1))[side]
        return pltpu.make_async_remote_copy(
            src_ref=proj, dst_ref=landing, send_sem=lead_send.at[side],
            recv_sem=lead_recv.at[side], device_id={"lead": index}, device_id_type=MESH,
        )

    def send_projection():
        @pl.when(jnp.logical_not(lead_last))
        def _():
            lead_copy(0).start()

        @pl.when(jnp.logical_not(lead_first))
        def _():
            lead_copy(1).start()

    def feature_conv(k):
        out = split_pairs(conv_pairs(xs, wf, k * ROWS, ROWS), ROWS, width)
        acc[pl.ds(k * ROWS, ROWS)] = jnp.stack(out, axis=1).reshape(ROWS, width, ch)

    def mix():
        @pl.when(jnp.logical_not(lead_first))
        def _():
            lead_copy(0).wait_recv()

        @pl.when(jnp.logical_not(lead_last))
        def _():
            lead_copy(1).wait_recv()

        @pl.when(lead_first)
        def _():
            prev[...] = jnp.zeros_like(prev)

        @pl.when(lead_last)
        def _():
            foll[...] = jnp.zeros_like(foll)

        now = hours_ref[lead]
        before = hours_ref[jnp.maximum(lead - 1, 0)]
        after = hours_ref[jnp.minimum(lead + 1, leads - 1)]

        def gain(later, earlier, absent):
            gap = jnp.full((1, ch), (later - earlier).astype(F32), F32)
            return jnp.where(absent, 0.0, jnp.exp(-0.5 * (gap - 1.0)))

        gain_prev = gain(now, before, lead_first)
        gain_next = gain(after, now, lead_last)
        value = gain_prev * dot(prev[...], wd[0])
        value = value + dot(proj[...], wd[1])
        value = value + gain_next * dot(foll[...], wd[2])
        mixed[...] = value.astype(BF16)

    total_rows = SLICE * groups

    def take_context(k):
        lane = lax.broadcasted_iota(jnp.int32, (total_rows, ch), 1)
        group = lax.rem(lax.broadcasted_iota(jnp.int32, (total_rows, ch), 0), groups)
        owner = owner_ref[lead]
        per_half = groups // HALVES
        for half in range(HALVES):
            low = jnp.where(owner < z, up_in[k, half], down_in[k, half])
            g = jnp.where(owner == z, c_ref[k, half], low).astype(F32)
            for j in range(per_half):
                at = half * per_half + j
                gt[pl.ds(at, SLICE, stride=groups), :] = g[:, j * ch : (j + 1) * ch]
        x = gt[...]
        y = pltpu.roll(x, ctx_ch, 1)
        back = jnp.where(group == 0, 0.0, pltpu.roll(y, 1, 0))
        ahead = jnp.where(group == groups - 1, 0.0, pltpu.roll(y, total_rows - 1, 0))
        beside = jnp.where(lane < ctx_ch, back, ahead)
        rows = pl.ds(1 + k * SLICE, SLICE)
        big_g[rows, :, :ch] = x.astype(BF16).reshape(SLICE, groups, ch)
        big_g[rows, :, ch:] = beside.astype(BF16).reshape(SLICE, groups, ch)

    def activate(row, count):
        size = count * groups
        lhs = [big_g[pl.ds(row + a, count)].reshape(size, 2 * ch) for a in range(3)]
        out = dot(jnp.concatenate(lhs, axis=1), wc[...])
        v = silu(out.reshape(2 * size, ch) + acc[pl.ds(row, count)].reshape(2 * size, ch))
        put_shifted(ys, v, row, count)

    def finish(row, count):
        o_ref[pl.ds(row, count)] = finished(f_ref, ys, ws, mixed, row, count)

    project()
    send_projection()
    shift_features()
    clear_edges()
    fetch(2).wait()
    pack_weights(wf, w1_ref)
    pack_context_weights()

    @pl.loop(0, EARLY)
    def _(k):
        feature_conv(k)

    for half in range(HALVES):
        fetch_context(half).wait()
    fetch(6).wait()
    fetch(7).wait()

    def pack_rest():
        for i in (3, 4, 5):
            fetch(i).wait()
        pack_weights(ws, w2_ref)
        pack_lead_weights()

    def wait_piece(copy, landed, c):
        for half in range(HALVES):
            copy(landed.at[c, half], c, half).wait_recv()

    edge = first | last

    @pl.when(edge)
    def _():
        @pl.loop(EARLY, chunks)
        def _(k):
            feature_conv(k)

        pack_rest()
        mix()

        def receive(c):
            @pl.when(first)
            def _():
                wait_piece(down_copy, down_in, c)

            @pl.when(last)
            def _():
                wait_piece(up_copy, up_in, c)

            take_context(c)

        @pl.loop(0, slices)
        def _(c):
            receive(c)

            @pl.when(c == 1)
            def _():
                activate(0, ROWS - 1)
                finish(0, ROWS - 2)

            @pl.when((c > 1) & (c < slices - 2) & (lax.rem(c, 2) == 1))
            def _():
                row = lax.div(c, 2) * ROWS
                activate(row - 1, ROWS)
                finish(row - 2, ROWS)


    @pl.when(jnp.logical_not(edge))
    def _():
        up_at, down_at = LAG * z, LAG * (n - 1 - z)
        ready_at = jnp.maximum(up_at, down_at)
        up_first = up_at >= down_at
        start_at = jnp.minimum(up_at, down_at)
        owner = owner_ref[lead]
        mine = owner == z

        def go(at, copy, landed, out):
            c, half = lax.div(at, HALVES), lax.rem(at, HALVES)

            @pl.when((at >= 0) & (at < pieces))
            def _():
                copy(landed.at[c, half], c, half).wait_recv()
                out[c, half] = jnp.where(mine, c_ref[c, half], landed[c, half])
                copy(out.at[c, half], c, half).start()

        @pl.loop(start_at, ready_at + pieces + LATE)
        def _(s):
            @pl.when(up_first)
            def _():
                go(s - up_at, up_copy, up_in, up_out)
                go(s - down_at, down_copy, down_in, down_out)

            @pl.when(jnp.logical_not(up_first))
            def _():
                go(s - down_at, down_copy, down_in, down_out)
                go(s - up_at, up_copy, up_in, up_out)

            t = s - start_at

            @pl.when(t <= chunks - EARLY + 1)
            def _():
                @pl.when(t < chunks - EARLY)
                def _():
                    feature_conv(t + EARLY)

                @pl.when(t == chunks - EARLY)
                def _():
                    pack_rest()

                @pl.when(t == chunks - EARLY + 1)
                def _():
                    mix()

            r = s - ready_at - LATE

            @pl.when(r >= 0)
            def _():
                take_context(r)

                @pl.when(r == 1)
                def _():
                    activate(0, ROWS - 1)

                @pl.when(r == 2)
                def _():
                    finish(0, ROWS - 2)

                odd = lax.rem(r, 2)
                row = (r - odd) * SLICE

                @pl.when((r > 2) & (r < slices - 2) & (odd == 1))
                def _():
                    activate(row - 1, ROWS)

                @pl.when((r > 2) & (odd == 0))
                def _():
                    finish(row - ROWS - 2, ROWS)

    activate(height - ROWS - 1, ROWS + 1)

    @pl.loop(0, slices)
    def _(c):
        for half in range(HALVES):
            @pl.when(jnp.logical_not(last))
            def _():
                up_copy(c_ref.at[c, half], c, half).wait_send()

            @pl.when(jnp.logical_not(first))
            def _():
                down_copy(c_ref.at[c, half], c, half).wait_send()

    @pl.when(jnp.logical_not(lead_last))
    def _():
        lead_copy(0).wait_send()

    @pl.when(jnp.logical_not(lead_first))
    def _():
        lead_copy(1).wait_send()


def per_device(
    features, context, owner, hours, w_first, w_second, w_lead_in, w_lead_mix, w_lead_out
):
    n, leads = lax.axis_size("patch"), lax.axis_size("lead")
    _, _, height, width, ch = features.shape
    temporal = w_lead_in.shape[1]
    merged = context.shape[3]
    cells = ROWS * width
    groups = merged // ch
    packs = ch // temporal
    packed_rows = height * width // packs
    vmem = pltpu.VMEM
    slices = height // SLICE
    pieces = HALVES * slices
    line = vmem((slices, HALVES, SLICE, merged // HALVES), BF16)
    hbm = pl.BlockSpec(memory_space=pl.ANY)
    dma = pltpu.SemaphoreType.DMA
    held = [
        vmem((height, width, ch), BF16),
        vmem((height, width, ch), BF16),
        vmem((3, height + 2, width, ch), BF16),
        vmem(((12 + packs // 2) * ch, 2 * ch), BF16),
        vmem((packed_rows, ch), BF16),
    ]
    most = pl.pallas_call(
        functools.partial(kernel, n, leads),
        out_shape=held,
        in_specs=[hbm] * 9,
        out_specs=[pl.BlockSpec(memory_space=pltpu.VMEM)] * len(held),
        scratch_shapes=[
            line,
            vmem(w_first.shape, BF16),
            vmem(w_second.shape, BF16),
            vmem((temporal, ch), BF16),
            vmem(w_lead_mix.shape, BF16),
            vmem(w_lead_out.shape, BF16),
            vmem((3, height + 2, width, ch), BF16),
            vmem((height, width, ch), F32),
            vmem((height + 2, groups, 2 * ch), BF16),
            vmem((SLICE * groups, ch), F32),
            vmem((12 * ch, 2 * ch), BF16),
            vmem((6 * ch, 2 * ch), BF16),
            vmem((3, ch, ch), BF16),
            vmem((ch, packs * ch), BF16),
            vmem((packed_rows, ch), BF16),
            vmem((packed_rows, ch), BF16),
            vmem((packed_rows, ch), BF16),
            line, line, line, line,
            pltpu.SMEM(owner.shape, jnp.int32), pltpu.SMEM(hours.shape, jnp.int32),
            dma((HALVES,)), dma((8,)),
            dma((pieces,)), dma((pieces,)), dma((pieces,)), dma((pieces,)), dma((2,)), dma((2,)),
        ],
        compiler_params=pltpu.CompilerParams(
            collective_id=0, has_side_effects=True, vmem_limit_bytes=LIMIT
        ),
    )(
        owner, hours, features[0, 0], context.reshape(slices, SLICE, merged),
        w_first, w_second, w_lead_in.T, w_lead_mix, w_lead_out,
    )
    out = pl.pallas_call(
        last_rows,
        out_shape=jax.ShapeDtypeStruct((height, width, ch), BF16),
        in_specs=[pl.BlockSpec(memory_space=pltpu.VMEM)] * len(held),
        out_specs=hbm,
        scratch_shapes=[vmem((ROWS + 2, width, ch), BF16), dma((2,))],
        compiler_params=pltpu.CompilerParams(vmem_limit_bytes=16 * 2**20),
    )(*most)
    return out[None, None]


def solution(mesh):
    placed = (
        P(("grp", "lead"), "patch", None, None, None),
        P("patch", ("grp", "lead"), None, None),
        P("grp"),
        P("grp"),
        P(),
        P(),
        P(),
        P(),
        P(),
    )
    return jax.shard_map(
        per_device,
        mesh=mesh,
        in_specs=placed,
        out_specs=P(("grp", "lead"), "patch", None, None, None),
        check_vma=False,
    )
```

```python
import functools

import jax
import jax.numpy as jnp
from jax import lax
from jax.experimental import pallas as pl
from jax.experimental.pallas import tpu as pltpu
from jax.sharding import PartitionSpec as P

MESH = pl.DeviceIdType.MESH
ROWS = 16
SLICE = 8
HALVES = 1
LAG = 5
LIMIT = 56 * 2**20
LATE = 5
PARTS = 4
EARLY = 3
F32 = jnp.float32
BF16 = jnp.bfloat16


def silu(v):
    return 0.5 * v * (1.0 + jnp.tanh(0.5 * v))


def dot(a, b):
    return jnp.dot(a, b, preferred_element_type=F32)


def conv_pairs(source, weights, row, count, more=()):
    width, ch = source.shape[2:]
    pairs = count // 2
    parts = [
        source[b, pl.ds(row, count + 2)].reshape(pairs + 1, 2, width, ch) for b in range(3)
    ]
    lhs = [
        parts[b][r // 2 : r // 2 + pairs, r % 2].reshape(pairs * width, ch)
        for r in range(4)
        for b in range(3)
    ]
    return dot(jnp.concatenate(lhs + list(more), axis=1), weights[...])

def split_pairs(out, count, width):
    ch = out.shape[1] // 2
    return [
        out[:, q * ch : (q + 1) * ch].reshape(count // 2, width, ch) for q in range(2)
    ]


def finished(f_ref, ys, ws, mixed, row, count):
    height, width, ch = f_ref.shape
    packs = height * width // mixed.shape[0]
    pairs, rows = count // 2, pl.ds(row, count)
    skip = row % packs if isinstance(row, int) else packs - 2
    skip = row % packs if isinstance(row, int) else packs - 2
    packed = (skip + count + packs - 1) // packs
    if isinstance(row, int):
        at = (row - skip) // packs * width
    else:
        at = pl.multiple_of(lax.div(row - skip, packs) * width, width)
    near = mixed[pl.ds(at, packed * width)]
    none = jnp.zeros((width, ch), BF16)
    more = []
    for turn in range(packs // 2):
        blocks = []
        for i in range(skip, skip + count, 2):
            m = i // packs
            hit = i % packs // 2 == turn
            blocks.append(near[m * width : (m + 1) * width] if hit else none)
        more.append(jnp.concatenate(blocks, axis=0))
    out = split_pairs(conv_pairs(ys, ws, row, count, more), count, width)
    own = f_ref[rows].reshape(pairs, 2, width, ch)
    results = []
    for q in range(2):
        results.append((own[:, q].astype(F32) + silu(out[q])).astype(BF16))
    return jnp.stack(results, axis=1).reshape(count, width, ch)


def last_rows(o_in, f_ref, ys, ws, mixed, out_hbm, rest, sem):
    height = f_ref.shape[0]
    start = height - ROWS - 2
    early = pltpu.make_async_copy(o_in.at[:start], out_hbm.at[:start], sem.at[0])
    early.start()
    rest[...] = finished(f_ref, ys, ws, mixed, start, ROWS + 2)
    late = pltpu.make_async_copy(rest, out_hbm.at[start:], sem.at[1])
    late.start()
    early.wait()
    late.wait()


def kernel(
    n, leads, owner_hbm, hours_hbm, f_hbm, c_hbm, w1_hbm, w2_hbm, wi_hbm, wm_hbm, wo_hbm, o_ref, f_ref, ys, ws, mixed,
    c_ref, w1_ref, w2_ref, wi_ref, wm_ref, wo_ref,
    xs, acc, big_g, gt, wf, wc, wd, wp, proj, prev, foll,
    up_in, down_in, up_out, down_out, owner_ref, hours_ref, small_sem, in_sem,
    up_send, up_recv, down_send, down_recv, lead_send, lead_recv,
):
    height, width, ch = f_ref.shape
    chunks = height // ROWS
    slices = height // SLICE
    half = ROWS // 2
    cells = ROWS * width
    part = c_ref.shape[3]
    ctx_ch = HALVES * part // width
    pieces = HALVES * slices
    per = ch // ctx_ch
    groups = width // per
    temporal = wi_ref.shape[0]
    packs = ch // temporal
    packed_rows = height * width // packs

    def fetch(i):
        source, target = (
            (f_hbm, f_ref), (wi_hbm, wi_ref), (w1_hbm, w1_ref), (w2_hbm, w2_ref),
            (wm_hbm, wm_ref), (wo_hbm, wo_ref), (owner_hbm, owner_ref), (hours_hbm, hours_ref),
        )[i]
        return pltpu.make_async_copy(source, target, in_sem.at[i])

    def fetch_context(half):
        return pltpu.make_async_copy(
            c_hbm.at[:, :, half * part : (half + 1) * part], c_ref.at[:, half], small_sem.at[half]
        )

    z = lax.axis_index("patch")
    lead = lax.axis_index("lead")
    first, last = z == 0, z == n - 1
    lead_first, lead_last = lead == 0, lead == leads - 1

    barrier = pltpu.get_barrier_semaphore()


    for cond, axis, index in (
        (jnp.logical_not(first), "patch", z - 1),
        (jnp.logical_not(last), "patch", z + 1),
        (jnp.logical_not(lead_first), "lead", lead - 1),
        (jnp.logical_not(lead_last), "lead", lead + 1),
    ):
        @pl.when(cond)
        def _(axis=axis, index=index):
            pl.semaphore_signal(barrier, inc=1, device_id={axis: index}, device_id_type=MESH)

    neighbours = (
        4
        - first.astype(jnp.int32)
        - last.astype(jnp.int32)
        - lead_first.astype(jnp.int32)
        - lead_last.astype(jnp.int32)
    )
    for i in (6, 7, 0, 1):
        fetch(i).start()
    for half in range(HALVES):
        fetch_context(half).start()
    for i in range(2, 6):
        fetch(i).start()

    pl.semaphore_wait(barrier, neighbours)

    def up_copy(src, c, half):
        at = HALVES * c + half
        return pltpu.make_async_remote_copy(
            src_ref=src, dst_ref=up_in.at[c, half], send_sem=up_send.at[at],
            recv_sem=up_recv.at[at], device_id={"patch": z + 1}, device_id_type=MESH,
        )

    def down_copy(src, c, half):
        at = HALVES * c + half
        return pltpu.make_async_remote_copy(
            src_ref=src, dst_ref=down_in.at[c, half], send_sem=down_send.at[at],
            recv_sem=down_recv.at[at], device_id={"patch": z - 1}, device_id_type=MESH,
        )

    @pl.when(first)
    def _():
        @pl.loop(0, slices)
        def _(c):
            for half in range(HALVES):
                up_copy(c_hbm.at[c, :, half * part : (half + 1) * part], c, half).start()

    @pl.when(last)
    def _():
        @pl.loop(0, slices)
        def _(c):
            for half in range(HALVES):
                down_copy(c_hbm.at[c, :, half * part : (half + 1) * part], c, half).start()

    def project():
        fetch(0).wait()
        fetch(1).wait()
        wp[...] = jnp.zeros_like(wp)
        parts = []
        whole = f_ref[...].reshape(height // packs, packs, width, ch)
        for q in range(packs):
            wp[q * temporal : (q + 1) * temporal, q * ch : (q + 1) * ch] = wi_ref[...]
            parts.append(whole[:, q].reshape(packed_rows, ch))
        total = lax.dot_general(
            jnp.concatenate(parts, axis=1), wp[...], (((1,), (1,)), ((), ())),
            preferred_element_type=F32,
        )
        proj[...] = total.astype(BF16)

    def pack_weights(target, source):
        zero = jnp.zeros((ch, ch), BF16)
        for r in range(4):
            for b in range(3):
                at = (3 * r + b) * ch
                for q in range(2):
                    a = r - q
                    block = source[3 * a + b, :ch, :] if 0 <= a <= 2 else zero
                    target[at : at + ch, q * ch : (q + 1) * ch] = block

    def pack_context_weights():
        small = jnp.zeros((ctx_ch, ch), BF16)
        for a in range(3):
            taps = [w1_ref[3 * a + b, ch:, :] for b in range(3)]
            for i, pair in enumerate(
                ((taps[1], taps[0]), (taps[2], taps[1]), (taps[0], small), (small, taps[2]))
            ):
                at = a * 4 * ctx_ch + i * ctx_ch
                for q in range(2):
                    wc[at : at + ctx_ch, q * ch : (q + 1) * ch] = pair[q]

    def pack_lead_weights():
        wd[...] = jnp.zeros_like(wd)
        ws[12 * ch :] = jnp.zeros((packs // 2 * ch, 2 * ch), BF16)
        for q in range(packs):
            at = slice(q * temporal, (q + 1) * temporal)
            for t in range(3):
                wd[t, at, at] = wm_ref[t]
            low = (12 + q // 2) * ch + q * temporal
            ws[low : low + temporal, q % 2 * ch : (q % 2 + 1) * ch] = wo_ref[...]

    def put_shifted(target, v, row, count):
        size = count * width
        col = lax.rem(lax.broadcasted_iota(jnp.int32, (size, ch), 0), width)
        left = jnp.where(col == 0, 0.0, pltpu.roll(v, 1, 0))
        right = jnp.where(col == width - 1, 0.0, pltpu.roll(v, size - 1, 0))
        for b, value in enumerate((left, v, right)):
            target[b, pl.ds(1 + row, count)] = value.astype(BF16).reshape(count, width, ch)

    def clear_edges():
        edge = jnp.zeros((width, ch), BF16)
        for target in (xs, ys):
            for b in range(3):
                target[b, 0] = edge
                target[b, height + 1] = edge
        big_g[0] = jnp.zeros(big_g.shape[1:], BF16)
        big_g[height + 1] = jnp.zeros(big_g.shape[1:], BF16)

    def shift_features():
        @pl.loop(0, chunks)
        def _(k):
            put_shifted(xs, f_ref[pl.ds(k * ROWS, ROWS)].reshape(cells, ch).astype(F32), k * ROWS, ROWS)

    def lead_copy(side):
        landing, index = ((prev, lead + 1), (foll, lead - 1))[side]
        return pltpu.make_async_remote_copy(
            src_ref=proj, dst_ref=landing, send_sem=lead_send.at[side],
            recv_sem=lead_recv.at[side], device_id={"lead": index}, device_id_type=MESH,
        )

    def send_projection():
        @pl.when(jnp.logical_not(lead_last))
        def _():
            lead_copy(0).start()

        @pl.when(jnp.logical_not(lead_first))
        def _():
            lead_copy(1).start()

    def feature_conv(k):
        out = split_pairs(conv_pairs(xs, wf, k * ROWS, ROWS), ROWS, width)
        acc[pl.ds(k * ROWS, ROWS)] = jnp.stack(out, axis=1).reshape(ROWS, width, ch)

    def mix_wait():
        @pl.when(jnp.logical_not(lead_first))
        def _():
            lead_copy(0).wait_recv()

        @pl.when(jnp.logical_not(lead_last))
        def _():
            lead_copy(1).wait_recv()

        @pl.when(lead_first)
        def _():
            prev[...] = jnp.zeros_like(prev)

        @pl.when(lead_last)
        def _():
            foll[...] = jnp.zeros_like(foll)

    def mix(i):
        now = hours_ref[lead]
        before = hours_ref[jnp.maximum(lead - 1, 0)]
        after = hours_ref[jnp.minimum(lead + 1, leads - 1)]

        def gain(later, earlier, absent):
            gap = jnp.full((1, ch), (later - earlier).astype(F32), F32)
            return jnp.where(absent, 0.0, jnp.exp(-0.5 * (gap - 1.0)))

        gain_prev = gain(now, before, lead_first)
        gain_next = gain(after, now, lead_last)
        size = packed_rows // PARTS
        rows = pl.ds(pl.multiple_of(i * size, size), size)
        value = gain_prev * dot(prev[rows], wd[0])
        value = value + dot(proj[rows], wd[1])
        value = value + gain_next * dot(foll[rows], wd[2])
        mixed[rows] = value.astype(BF16)

    total_rows = SLICE * groups

    def take_context(k):
        lane = lax.broadcasted_iota(jnp.int32, (total_rows, ch), 1)
        group = lax.rem(lax.broadcasted_iota(jnp.int32, (total_rows, ch), 0), groups)
        owner = owner_ref[lead]
        per_half = groups // HALVES
        for half in range(HALVES):
            low = jnp.where(owner < z, up_in[k, half], down_in[k, half])
            g = jnp.where(owner == z, c_ref[k, half], low).astype(F32)
            for j in range(per_half):
                at = half * per_half + j
                gt[pl.ds(at, SLICE, stride=groups), :] = g[:, j * ch : (j + 1) * ch]
        x = gt[...]
        y = pltpu.roll(x, ctx_ch, 1)
        back = jnp.where(group == 0, 0.0, pltpu.roll(y, 1, 0))
        ahead = jnp.where(group == groups - 1, 0.0, pltpu.roll(y, total_rows - 1, 0))
        beside = jnp.where(lane < ctx_ch, back, ahead)
        rows = pl.ds(1 + k * SLICE, SLICE)
        big_g[rows, :, :ch] = x.astype(BF16).reshape(SLICE, groups, ch)
        big_g[rows, :, ch:] = beside.astype(BF16).reshape(SLICE, groups, ch)

    def activate(row, count):
        size = count * groups
        lhs = [big_g[pl.ds(row + a, count)].reshape(size, 2 * ch) for a in range(3)]
        out = dot(jnp.concatenate(lhs, axis=1), wc[...])
        v = silu(out.reshape(2 * size, ch) + acc[pl.ds(row, count)].reshape(2 * size, ch))
        put_shifted(ys, v, row, count)

    def finish(row, count):
        o_ref[pl.ds(row, count)] = finished(f_ref, ys, ws, mixed, row, count)

    project()
    send_projection()
    shift_features()
    clear_edges()
    fetch(2).wait()
    pack_weights(wf, w1_ref)
    pack_context_weights()

    @pl.loop(0, EARLY)
    def _(k):
        feature_conv(k)

    for half in range(HALVES):
        fetch_context(half).wait()
    fetch(6).wait()
    fetch(7).wait()

    def pack_rest():
        for i in (3, 4, 5):
            fetch(i).wait()
        pack_weights(ws, w2_ref)
        pack_lead_weights()

    def wait_piece(copy, landed, c):
        for half in range(HALVES):
            copy(landed.at[c, half], c, half).wait_recv()

    edge = first | last

    @pl.when(edge)
    def _():
        @pl.loop(EARLY, chunks)
        def _(k):
            feature_conv(k)

        pack_rest()
        mix_wait()

        @pl.loop(0, PARTS)
        def _(i):
            mix(i)


        def receive(c):
            @pl.when(first)
            def _():
                wait_piece(down_copy, down_in, c)

            @pl.when(last)
            def _():
                wait_piece(up_copy, up_in, c)

            take_context(c)

        @pl.loop(0, slices)
        def _(c):
            receive(c)

            @pl.when(c == 1)
            def _():
                activate(0, ROWS - 1)
                finish(0, ROWS - 2)

            @pl.when((c > 1) & (c < slices - 2) & (lax.rem(c, 2) == 1))
            def _():
                row = lax.div(c, 2) * ROWS
                activate(row - 1, ROWS)
                finish(row - 2, ROWS)


    @pl.when(jnp.logical_not(edge))
    def _():
        up_at, down_at = LAG * z, LAG * (n - 1 - z)
        ready_at = jnp.maximum(up_at, down_at)
        up_first = up_at >= down_at
        start_at = jnp.minimum(up_at, down_at)
        owner = owner_ref[lead]
        mine = owner == z

        def go(at, copy, landed, out):
            c, half = lax.div(at, HALVES), lax.rem(at, HALVES)

            @pl.when((at >= 0) & (at < pieces))
            def _():
                copy(landed.at[c, half], c, half).wait_recv()
                out[c, half] = jnp.where(mine, c_ref[c, half], landed[c, half])
                copy(out.at[c, half], c, half).start()

        @pl.loop(start_at, ready_at + pieces + LATE)
        def _(s):
            @pl.when(up_first)
            def _():
                go(s - up_at, up_copy, up_in, up_out)
                go(s - down_at, down_copy, down_in, down_out)

            @pl.when(jnp.logical_not(up_first))
            def _():
                go(s - down_at, down_copy, down_in, down_out)
                go(s - up_at, up_copy, up_in, up_out)

            t = s - start_at

            mix_at = chunks - EARLY + 1

            @pl.when(t < mix_at + PARTS)
            def _():
                @pl.when(t < chunks - EARLY)
                def _():
                    feature_conv(t + EARLY)

                @pl.when(t == chunks - EARLY)
                def _():
                    pack_rest()

                @pl.when(t == mix_at)
                def _():
                    mix_wait()

                @pl.when(t >= mix_at)
                def _():
                    mix(t - mix_at)

            r = s - ready_at - LATE

            @pl.when(r >= 0)
            def _():
                take_context(r)

                @pl.when(r == 1)
                def _():
                    activate(0, ROWS - 1)

                @pl.when(r == 2)
                def _():
                    finish(0, ROWS - 2)

                odd = lax.rem(r, 2)
                row = (r - odd) * SLICE

                @pl.when((r > 2) & (r < slices - 2) & (odd == 1))
                def _():
                    activate(row - 1, ROWS)

                @pl.when((r > 2) & (odd == 0))
                def _():
                    finish(row - ROWS - 2, ROWS)

    activate(height - ROWS - 1, ROWS + 1)

    @pl.loop(0, slices)
    def _(c):
        for half in range(HALVES):
            @pl.when(jnp.logical_not(last))
            def _():
                up_copy(c_ref.at[c, half], c, half).wait_send()

            @pl.when(jnp.logical_not(first))
            def _():
                down_copy(c_ref.at[c, half], c, half).wait_send()

    @pl.when(jnp.logical_not(lead_last))
    def _():
        lead_copy(0).wait_send()

    @pl.when(jnp.logical_not(lead_first))
    def _():
        lead_copy(1).wait_send()


def per_device(
    features, context, owner, hours, w_first, w_second, w_lead_in, w_lead_mix, w_lead_out
):
    n, leads = lax.axis_size("patch"), lax.axis_size("lead")
    _, _, height, width, ch = features.shape
    temporal = w_lead_in.shape[1]
    merged = context.shape[3]
    cells = ROWS * width
    groups = merged // ch
    packs = ch // temporal
    packed_rows = height * width // packs
    vmem = pltpu.VMEM
    slices = height // SLICE
    pieces = HALVES * slices
    line = vmem((slices, HALVES, SLICE, merged // HALVES), BF16)
    hbm = pl.BlockSpec(memory_space=pl.ANY)
    dma = pltpu.SemaphoreType.DMA
    held = [
        vmem((height, width, ch), BF16),
        vmem((height, width, ch), BF16),
        vmem((3, height + 2, width, ch), BF16),
        vmem(((12 + packs // 2) * ch, 2 * ch), BF16),
        vmem((packed_rows, ch), BF16),
    ]
    most = pl.pallas_call(
        functools.partial(kernel, n, leads),
        out_shape=held,
        in_specs=[hbm] * 9,
        out_specs=[pl.BlockSpec(memory_space=pltpu.VMEM)] * len(held),
        scratch_shapes=[
            line,
            vmem(w_first.shape, BF16),
            vmem(w_second.shape, BF16),
            vmem((temporal, ch), BF16),
            vmem(w_lead_mix.shape, BF16),
            vmem(w_lead_out.shape, BF16),
            vmem((3, height + 2, width, ch), BF16),
            vmem((height, width, ch), F32),
            vmem((height + 2, groups, 2 * ch), BF16),
            vmem((SLICE * groups, ch), F32),
            vmem((12 * ch, 2 * ch), BF16),
            vmem((6 * ch, 2 * ch), BF16),
            vmem((3, ch, ch), BF16),
            vmem((ch, packs * ch), BF16),
            vmem((packed_rows, ch), BF16),
            vmem((packed_rows, ch), BF16),
            vmem((packed_rows, ch), BF16),
            line, line, line, line,
            pltpu.SMEM(owner.shape, jnp.int32), pltpu.SMEM(hours.shape, jnp.int32),
            dma((HALVES,)), dma((8,)),
            dma((pieces,)), dma((pieces,)), dma((pieces,)), dma((pieces,)), dma((2,)), dma((2,)),
        ],
        compiler_params=pltpu.CompilerParams(
            collective_id=0, has_side_effects=True, vmem_limit_bytes=LIMIT
        ),
    )(
        owner, hours, features[0, 0], context.reshape(slices, SLICE, merged),
        w_first, w_second, w_lead_in.T, w_lead_mix, w_lead_out,
    )
    out = pl.pallas_call(
        last_rows,
        out_shape=jax.ShapeDtypeStruct((height, width, ch), BF16),
        in_specs=[pl.BlockSpec(memory_space=pltpu.VMEM)] * len(held),
        out_specs=hbm,
        scratch_shapes=[vmem((ROWS + 2, width, ch), BF16), dma((2,))],
        compiler_params=pltpu.CompilerParams(vmem_limit_bytes=16 * 2**20),
    )(*most)
    return out[None, None]


def solution(mesh):
    placed = (
        P(("grp", "lead"), "patch", None, None, None),
        P("patch", ("grp", "lead"), None, None),
        P("grp"),
        P("grp"),
        P(),
        P(),
        P(),
        P(),
        P(),
    )
    return jax.shard_map(
        per_device,
        mesh=mesh,
        in_specs=placed,
        out_specs=P(("grp", "lead"), "patch", None, None, None),
        check_vma=False,
    )
```

```python
import functools

import jax
import jax.numpy as jnp
from jax import lax
from jax.experimental import pallas as pl
from jax.experimental.pallas import tpu as pltpu
from jax.sharding import PartitionSpec as P

MESH = pl.DeviceIdType.MESH
ROWS = 16
SLICE = 8
HALVES = 1
LAG = 5
LIMIT = 56 * 2**20
LATE = 5
PARTS = 4
EARLY = 3
F32 = jnp.float32
BF16 = jnp.bfloat16


def silu(v):
    return 0.5 * v * (1.0 + jnp.tanh(0.5 * v))


def dot(a, b):
    return jnp.dot(a, b, preferred_element_type=F32)


def conv_pairs(source, weights, row, count, more=()):
    width, ch = source.shape[2:]
    pairs = count // 2
    parts = [
        source[b, pl.ds(row, count + 2)].reshape(pairs + 1, 2, width, ch) for b in range(3)
    ]
    lhs = [
        parts[b][r // 2 : r // 2 + pairs, r % 2].reshape(pairs * width, ch)
        for r in range(4)
        for b in range(3)
    ]
    return dot(jnp.concatenate(lhs + list(more), axis=1), weights[...])

def split_pairs(out, count, width):
    ch = out.shape[1] // 2
    return [
        out[:, q * ch : (q + 1) * ch].reshape(count // 2, width, ch) for q in range(2)
    ]


def finished(f_ref, ys, ws, mixed, row, count):
    height, width, ch = f_ref.shape
    packs = height * width // mixed.shape[0]
    pairs, rows = count // 2, pl.ds(row, count)
    skip = row % packs if isinstance(row, int) else packs - 2
    skip = row % packs if isinstance(row, int) else packs - 2
    packed = (skip + count + packs - 1) // packs
    if isinstance(row, int):
        at = (row - skip) // packs * width
    else:
        at = pl.multiple_of(lax.div(row - skip, packs) * width, width)
    near = mixed[pl.ds(at, packed * width)]
    none = jnp.zeros((width, ch), BF16)
    more = []
    for turn in range(packs // 2):
        blocks = []
        for i in range(skip, skip + count, 2):
            m = i // packs
            hit = i % packs // 2 == turn
            blocks.append(near[m * width : (m + 1) * width] if hit else none)
        more.append(jnp.concatenate(blocks, axis=0))
    out = split_pairs(conv_pairs(ys, ws, row, count, more), count, width)
    own = f_ref[rows].reshape(pairs, 2, width, ch)
    results = []
    for q in range(2):
        results.append((own[:, q].astype(F32) + silu(out[q])).astype(BF16))
    return jnp.stack(results, axis=1).reshape(count, width, ch)


def last_rows(o_in, f_ref, ys, ws, mixed, out_hbm, rest, sem):
    height = f_ref.shape[0]
    start = height - ROWS - 2
    early = pltpu.make_async_copy(o_in.at[:start], out_hbm.at[:start], sem.at[0])
    early.start()
    rest[...] = finished(f_ref, ys, ws, mixed, start, ROWS + 2)
    late = pltpu.make_async_copy(rest, out_hbm.at[start:], sem.at[1])
    late.start()
    early.wait()
    late.wait()


def kernel(
    n, leads, owner_hbm, hours_hbm, f_hbm, c_hbm, w1_hbm, w2_hbm, wi_hbm, wm_hbm, wo_hbm, o_ref, f_ref, ys, ws, mixed,
    c_ref, w1_ref, w2_ref, wi_ref, wm_ref, wo_ref,
    xs, acc, big_g, gt, wf, wc, wd, wp, proj, prev, foll,
    up_in, down_in, up_out, down_out, owner_ref, hours_ref, small_sem, in_sem,
    up_send, up_recv, down_send, down_recv, lead_send, lead_recv,
):
    height, width, ch = f_ref.shape
    chunks = height // ROWS
    slices = height // SLICE
    half = ROWS // 2
    cells = ROWS * width
    part = c_ref.shape[3]
    ctx_ch = HALVES * part // width
    pieces = HALVES * slices
    per = ch // ctx_ch
    groups = width // per
    temporal = wi_ref.shape[0]
    packs = ch // temporal
    packed_rows = height * width // packs

    def fetch(i):
        source, target = (
            (f_hbm, f_ref), (wi_hbm, wi_ref), (w1_hbm, w1_ref), (w2_hbm, w2_ref),
            (wm_hbm, wm_ref), (wo_hbm, wo_ref), (owner_hbm, owner_ref), (hours_hbm, hours_ref),
        )[i]
        return pltpu.make_async_copy(source, target, in_sem.at[i])

    def fetch_context(half):
        return pltpu.make_async_copy(
            c_hbm.at[:, :, half * part : (half + 1) * part], c_ref.at[:, half], small_sem.at[half]
        )

    z = lax.axis_index("patch")
    lead = lax.axis_index("lead")
    first, last = z == 0, z == n - 1
    lead_first, lead_last = lead == 0, lead == leads - 1

    barrier = pltpu.get_barrier_semaphore()


    for cond, axis, index in (
        (jnp.logical_not(first), "patch", z - 1),
        (jnp.logical_not(last), "patch", z + 1),
        (jnp.logical_not(lead_first), "lead", lead - 1),
        (jnp.logical_not(lead_last), "lead", lead + 1),
    ):
        @pl.when(cond)
        def _(axis=axis, index=index):
            pl.semaphore_signal(barrier, inc=1, device_id={axis: index}, device_id_type=MESH)

    neighbours = (
        4
        - first.astype(jnp.int32)
        - last.astype(jnp.int32)
        - lead_first.astype(jnp.int32)
        - lead_last.astype(jnp.int32)
    )
    for i in (6, 7, 0, 1):
        fetch(i).start()
    for half in range(HALVES):
        fetch_context(half).start()
    pl.semaphore_wait(barrier, neighbours)

    def up_copy(src, c, half):
        at = HALVES * c + half
        return pltpu.make_async_remote_copy(
            src_ref=src, dst_ref=up_in.at[c, half], send_sem=up_send.at[at],
            recv_sem=up_recv.at[at], device_id={"patch": z + 1}, device_id_type=MESH,
        )

    def down_copy(src, c, half):
        at = HALVES * c + half
        return pltpu.make_async_remote_copy(
            src_ref=src, dst_ref=down_in.at[c, half], send_sem=down_send.at[at],
            recv_sem=down_recv.at[at], device_id={"patch": z - 1}, device_id_type=MESH,
        )

    @pl.when(first)
    def _():
        @pl.loop(0, slices)
        def _(c):
            for half in range(HALVES):
                up_copy(c_hbm.at[c, :, half * part : (half + 1) * part], c, half).start()

    @pl.when(last)
    def _():
        @pl.loop(0, slices)
        def _(c):
            for half in range(HALVES):
                down_copy(c_hbm.at[c, :, half * part : (half + 1) * part], c, half).start()

    for i in range(2, 6):
        fetch(i).start()

    def project():
        fetch(0).wait()
        fetch(1).wait()
        wp[...] = jnp.zeros_like(wp)
        parts = []
        whole = f_ref[...].reshape(height // packs, packs, width, ch)
        for q in range(packs):
            wp[q * temporal : (q + 1) * temporal, q * ch : (q + 1) * ch] = wi_ref[...]
            parts.append(whole[:, q].reshape(packed_rows, ch))
        total = lax.dot_general(
            jnp.concatenate(parts, axis=1), wp[...], (((1,), (1,)), ((), ())),
            preferred_element_type=F32,
        )
        proj[...] = total.astype(BF16)

    def pack_weights(target, source):
        zero = jnp.zeros((ch, ch), BF16)
        for r in range(4):
            for b in range(3):
                at = (3 * r + b) * ch
                for q in range(2):
                    a = r - q
                    block = source[3 * a + b, :ch, :] if 0 <= a <= 2 else zero
                    target[at : at + ch, q * ch : (q + 1) * ch] = block

    def pack_context_weights():
        small = jnp.zeros((ctx_ch, ch), BF16)
        for a in range(3):
            taps = [w1_ref[3 * a + b, ch:, :] for b in range(3)]
            for i, pair in enumerate(
                ((taps[1], taps[0]), (taps[2], taps[1]), (taps[0], small), (small, taps[2]))
            ):
                at = a * 4 * ctx_ch + i * ctx_ch
                for q in range(2):
                    wc[at : at + ctx_ch, q * ch : (q + 1) * ch] = pair[q]

    def pack_lead_weights():
        wd[...] = jnp.zeros_like(wd)
        ws[12 * ch :] = jnp.zeros((packs // 2 * ch, 2 * ch), BF16)
        for q in range(packs):
            at = slice(q * temporal, (q + 1) * temporal)
            for t in range(3):
                wd[t, at, at] = wm_ref[t]
            low = (12 + q // 2) * ch + q * temporal
            ws[low : low + temporal, q % 2 * ch : (q % 2 + 1) * ch] = wo_ref[...]

    def put_shifted(target, v, row, count):
        size = count * width
        col = lax.rem(lax.broadcasted_iota(jnp.int32, (size, ch), 0), width)
        left = jnp.where(col == 0, 0.0, pltpu.roll(v, 1, 0))
        right = jnp.where(col == width - 1, 0.0, pltpu.roll(v, size - 1, 0))
        for b, value in enumerate((left, v, right)):
            target[b, pl.ds(1 + row, count)] = value.astype(BF16).reshape(count, width, ch)

    def clear_edges():
        edge = jnp.zeros((width, ch), BF16)
        for target in (xs, ys):
            for b in range(3):
                target[b, 0] = edge
                target[b, height + 1] = edge
        big_g[0] = jnp.zeros(big_g.shape[1:], BF16)
        big_g[height + 1] = jnp.zeros(big_g.shape[1:], BF16)

    def shift_features():
        @pl.loop(0, chunks)
        def _(k):
            put_shifted(xs, f_ref[pl.ds(k * ROWS, ROWS)].reshape(cells, ch).astype(F32), k * ROWS, ROWS)

    def lead_copy(side):
        landing, index = ((prev, lead + 1), (foll, lead - 1))[side]
        return pltpu.make_async_remote_copy(
            src_ref=proj, dst_ref=landing, send_sem=lead_send.at[side],
            recv_sem=lead_recv.at[side], device_id={"lead": index}, device_id_type=MESH,
        )

    def send_projection():
        @pl.when(jnp.logical_not(lead_last))
        def _():
            lead_copy(0).start()

        @pl.when(jnp.logical_not(lead_first))
        def _():
            lead_copy(1).start()

    def feature_conv(k):
        out = split_pairs(conv_pairs(xs, wf, k * ROWS, ROWS), ROWS, width)
        acc[pl.ds(k * ROWS, ROWS)] = jnp.stack(out, axis=1).reshape(ROWS, width, ch)

    def mix_wait():
        @pl.when(jnp.logical_not(lead_first))
        def _():
            lead_copy(0).wait_recv()

        @pl.when(jnp.logical_not(lead_last))
        def _():
            lead_copy(1).wait_recv()

        @pl.when(lead_first)
        def _():
            prev[...] = jnp.zeros_like(prev)

        @pl.when(lead_last)
        def _():
            foll[...] = jnp.zeros_like(foll)

    def mix(i):
        now = hours_ref[lead]
        before = hours_ref[jnp.maximum(lead - 1, 0)]
        after = hours_ref[jnp.minimum(lead + 1, leads - 1)]

        def gain(later, earlier, absent):
            gap = jnp.full((1, ch), (later - earlier).astype(F32), F32)
            return jnp.where(absent, 0.0, jnp.exp(-0.5 * (gap - 1.0)))

        gain_prev = gain(now, before, lead_first)
        gain_next = gain(after, now, lead_last)
        size = packed_rows // PARTS
        rows = pl.ds(pl.multiple_of(i * size, size), size)
        value = gain_prev * dot(prev[rows], wd[0])
        value = value + dot(proj[rows], wd[1])
        value = value + gain_next * dot(foll[rows], wd[2])
        mixed[rows] = value.astype(BF16)

    total_rows = SLICE * groups

    def take_context(k):
        lane = lax.broadcasted_iota(jnp.int32, (total_rows, ch), 1)
        group = lax.rem(lax.broadcasted_iota(jnp.int32, (total_rows, ch), 0), groups)
        owner = owner_ref[lead]
        per_half = groups // HALVES
        for half in range(HALVES):
            low = jnp.where(owner < z, up_in[k, half], down_in[k, half])
            g = jnp.where(owner == z, c_ref[k, half], low).astype(F32)
            for j in range(per_half):
                at = half * per_half + j
                gt[pl.ds(at, SLICE, stride=groups), :] = g[:, j * ch : (j + 1) * ch]
        x = gt[...]
        y = pltpu.roll(x, ctx_ch, 1)
        back = jnp.where(group == 0, 0.0, pltpu.roll(y, 1, 0))
        ahead = jnp.where(group == groups - 1, 0.0, pltpu.roll(y, total_rows - 1, 0))
        beside = jnp.where(lane < ctx_ch, back, ahead)
        rows = pl.ds(1 + k * SLICE, SLICE)
        big_g[rows, :, :ch] = x.astype(BF16).reshape(SLICE, groups, ch)
        big_g[rows, :, ch:] = beside.astype(BF16).reshape(SLICE, groups, ch)

    def activate(row, count):
        size = count * groups
        lhs = [big_g[pl.ds(row + a, count)].reshape(size, 2 * ch) for a in range(3)]
        out = dot(jnp.concatenate(lhs, axis=1), wc[...])
        v = silu(out.reshape(2 * size, ch) + acc[pl.ds(row, count)].reshape(2 * size, ch))
        put_shifted(ys, v, row, count)

    def finish(row, count):
        o_ref[pl.ds(row, count)] = finished(f_ref, ys, ws, mixed, row, count)

    project()
    send_projection()
    shift_features()
    clear_edges()
    fetch(2).wait()
    pack_weights(wf, w1_ref)
    pack_context_weights()

    @pl.loop(0, EARLY)
    def _(k):
        feature_conv(k)

    for half in range(HALVES):
        fetch_context(half).wait()
    fetch(6).wait()
    fetch(7).wait()

    def pack_rest():
        for i in (3, 4, 5):
            fetch(i).wait()
        pack_weights(ws, w2_ref)
        pack_lead_weights()

    def wait_piece(copy, landed, c):
        for half in range(HALVES):
            copy(landed.at[c, half], c, half).wait_recv()

    edge = first | last

    @pl.when(edge)
    def _():
        @pl.loop(EARLY, chunks)
        def _(k):
            feature_conv(k)

        pack_rest()
        mix_wait()

        @pl.loop(0, PARTS)
        def _(i):
            mix(i)


        def receive(c):
            @pl.when(first)
            def _():
                wait_piece(down_copy, down_in, c)

            @pl.when(last)
            def _():
                wait_piece(up_copy, up_in, c)

            take_context(c)

        @pl.loop(0, slices)
        def _(c):
            receive(c)

            @pl.when(c == 1)
            def _():
                activate(0, ROWS - 1)
                finish(0, ROWS - 2)

            @pl.when((c > 1) & (c < slices - 2) & (lax.rem(c, 2) == 1))
            def _():
                row = lax.div(c, 2) * ROWS
                activate(row - 1, ROWS)
                finish(row - 2, ROWS)


    @pl.when(jnp.logical_not(edge))
    def _():
        up_at, down_at = LAG * z, LAG * (n - 1 - z)
        ready_at = jnp.maximum(up_at, down_at)
        up_first = up_at >= down_at
        start_at = jnp.minimum(up_at, down_at)
        owner = owner_ref[lead]
        mine = owner == z

        def go(at, copy, landed, out):
            c, half = lax.div(at, HALVES), lax.rem(at, HALVES)

            @pl.when((at >= 0) & (at < pieces))
            def _():
                copy(landed.at[c, half], c, half).wait_recv()
                out[c, half] = jnp.where(mine, c_ref[c, half], landed[c, half])
                copy(out.at[c, half], c, half).start()

        @pl.loop(start_at, ready_at + pieces + LATE)
        def _(s):
            @pl.when(up_first)
            def _():
                go(s - up_at, up_copy, up_in, up_out)
                go(s - down_at, down_copy, down_in, down_out)

            @pl.when(jnp.logical_not(up_first))
            def _():
                go(s - down_at, down_copy, down_in, down_out)
                go(s - up_at, up_copy, up_in, up_out)

            t = s - start_at

            mix_at = chunks - EARLY + 1

            @pl.when(t < mix_at + PARTS)
            def _():
                @pl.when(t < chunks - EARLY)
                def _():
                    feature_conv(t + EARLY)

                @pl.when(t == chunks - EARLY)
                def _():
                    pack_rest()

                @pl.when(t == mix_at)
                def _():
                    mix_wait()

                @pl.when(t >= mix_at)
                def _():
                    mix(t - mix_at)

            r = s - ready_at - LATE

            @pl.when(r >= 0)
            def _():
                take_context(r)

                @pl.when(r == 1)
                def _():
                    activate(0, ROWS - 1)

                @pl.when(r == 2)
                def _():
                    finish(0, ROWS - 2)

                odd = lax.rem(r, 2)
                row = (r - odd) * SLICE

                @pl.when((r > 2) & (r < slices - 2) & (odd == 1))
                def _():
                    activate(row - 1, ROWS)

                @pl.when((r > 2) & (odd == 0))
                def _():
                    finish(row - ROWS - 2, ROWS)

    activate(height - ROWS - 1, ROWS + 1)

    @pl.loop(0, slices)
    def _(c):
        for half in range(HALVES):
            @pl.when(jnp.logical_not(last))
            def _():
                up_copy(c_ref.at[c, half], c, half).wait_send()

            @pl.when(jnp.logical_not(first))
            def _():
                down_copy(c_ref.at[c, half], c, half).wait_send()

    @pl.when(jnp.logical_not(lead_last))
    def _():
        lead_copy(0).wait_send()

    @pl.when(jnp.logical_not(lead_first))
    def _():
        lead_copy(1).wait_send()


def per_device(
    features, context, owner, hours, w_first, w_second, w_lead_in, w_lead_mix, w_lead_out
):
    n, leads = lax.axis_size("patch"), lax.axis_size("lead")
    _, _, height, width, ch = features.shape
    temporal = w_lead_in.shape[1]
    merged = context.shape[3]
    cells = ROWS * width
    groups = merged // ch
    packs = ch // temporal
    packed_rows = height * width // packs
    vmem = pltpu.VMEM
    slices = height // SLICE
    pieces = HALVES * slices
    line = vmem((slices, HALVES, SLICE, merged // HALVES), BF16)
    hbm = pl.BlockSpec(memory_space=pl.ANY)
    dma = pltpu.SemaphoreType.DMA
    held = [
        vmem((height, width, ch), BF16),
        vmem((height, width, ch), BF16),
        vmem((3, height + 2, width, ch), BF16),
        vmem(((12 + packs // 2) * ch, 2 * ch), BF16),
        vmem((packed_rows, ch), BF16),
    ]
    most = pl.pallas_call(
        functools.partial(kernel, n, leads),
        out_shape=held,
        in_specs=[hbm] * 9,
        out_specs=[pl.BlockSpec(memory_space=pltpu.VMEM)] * len(held),
        scratch_shapes=[
            line,
            vmem(w_first.shape, BF16),
            vmem(w_second.shape, BF16),
            vmem((temporal, ch), BF16),
            vmem(w_lead_mix.shape, BF16),
            vmem(w_lead_out.shape, BF16),
            vmem((3, height + 2, width, ch), BF16),
            vmem((height, width, ch), F32),
            vmem((height + 2, groups, 2 * ch), BF16),
            vmem((SLICE * groups, ch), F32),
            vmem((12 * ch, 2 * ch), BF16),
            vmem((6 * ch, 2 * ch), BF16),
            vmem((3, ch, ch), BF16),
            vmem((ch, packs * ch), BF16),
            vmem((packed_rows, ch), BF16),
            vmem((packed_rows, ch), BF16),
            vmem((packed_rows, ch), BF16),
            line, line, line, line,
            pltpu.SMEM(owner.shape, jnp.int32), pltpu.SMEM(hours.shape, jnp.int32),
            dma((HALVES,)), dma((8,)),
            dma((pieces,)), dma((pieces,)), dma((pieces,)), dma((pieces,)), dma((2,)), dma((2,)),
        ],
        compiler_params=pltpu.CompilerParams(
            collective_id=0, has_side_effects=True, vmem_limit_bytes=LIMIT
        ),
    )(
        owner, hours, features[0, 0], context.reshape(slices, SLICE, merged),
        w_first, w_second, w_lead_in.T, w_lead_mix, w_lead_out,
    )
    out = pl.pallas_call(
        last_rows,
        out_shape=jax.ShapeDtypeStruct((height, width, ch), BF16),
        in_specs=[pl.BlockSpec(memory_space=pltpu.VMEM)] * len(held),
        out_specs=hbm,
        scratch_shapes=[vmem((ROWS + 2, width, ch), BF16), dma((2,))],
        compiler_params=pltpu.CompilerParams(vmem_limit_bytes=16 * 2**20),
    )(*most)
    return out[None, None]


def solution(mesh):
    placed = (
        P(("grp", "lead"), "patch", None, None, None),
        P("patch", ("grp", "lead"), None, None),
        P("grp"),
        P("grp"),
        P(),
        P(),
        P(),
        P(),
        P(),
    )
    return jax.shard_map(
        per_device,
        mesh=mesh,
        in_specs=placed,
        out_specs=P(("grp", "lead"), "patch", None, None, None),
        check_vma=False,
    )
```

```python
import functools

import jax
import jax.numpy as jnp
from jax import lax
from jax.experimental import pallas as pl
from jax.experimental.pallas import tpu as pltpu
from jax.sharding import PartitionSpec as P

MESH = pl.DeviceIdType.MESH
ROWS = 16
SLICE = 8
HALVES = 1
LAG = 5
LIMIT = 56 * 2**20
LATE = 6
PARTS = 4
EARLY = 3
F32 = jnp.float32
BF16 = jnp.bfloat16


def silu(v):
    return 0.5 * v * (1.0 + jnp.tanh(0.5 * v))


def dot(a, b):
    return jnp.dot(a, b, preferred_element_type=F32)


def conv_pairs(source, weights, row, count, more=()):
    width, ch = source.shape[2:]
    pairs = count // 2
    parts = [
        source[b, pl.ds(row, count + 2)].reshape(pairs + 1, 2, width, ch) for b in range(3)
    ]
    lhs = [
        parts[b][r // 2 : r // 2 + pairs, r % 2].reshape(pairs * width, ch)
        for r in range(4)
        for b in range(3)
    ]
    return dot(jnp.concatenate(lhs + list(more), axis=1), weights[...])

def split_pairs(out, count, width):
    ch = out.shape[1] // 2
    return [
        out[:, q * ch : (q + 1) * ch].reshape(count // 2, width, ch) for q in range(2)
    ]


def finished(f_ref, ys, ws, mixed, row, count):
    height, width, ch = f_ref.shape
    packs = height * width // mixed.shape[0]
    pairs, rows = count // 2, pl.ds(row, count)
    skip = row % packs if isinstance(row, int) else packs - 2
    skip = row % packs if isinstance(row, int) else packs - 2
    packed = (skip + count + packs - 1) // packs
    if isinstance(row, int):
        at = (row - skip) // packs * width
    else:
        at = pl.multiple_of(lax.div(row - skip, packs) * width, width)
    near = mixed[pl.ds(at, packed * width)]
    none = jnp.zeros((width, ch), BF16)
    more = []
    for turn in range(packs // 2):
        blocks = []
        for i in range(skip, skip + count, 2):
            m = i // packs
            hit = i % packs // 2 == turn
            blocks.append(near[m * width : (m + 1) * width] if hit else none)
        more.append(jnp.concatenate(blocks, axis=0))
    out = split_pairs(conv_pairs(ys, ws, row, count, more), count, width)
    own = f_ref[rows].reshape(pairs, 2, width, ch)
    results = []
    for q in range(2):
        results.append((own[:, q].astype(F32) + silu(out[q])).astype(BF16))
    return jnp.stack(results, axis=1).reshape(count, width, ch)


def last_rows(o_in, f_ref, ys, ws, mixed, out_hbm, rest, sem):
    height = f_ref.shape[0]
    start = height - ROWS - 2
    early = pltpu.make_async_copy(o_in.at[:start], out_hbm.at[:start], sem.at[0])
    early.start()
    rest[...] = finished(f_ref, ys, ws, mixed, start, ROWS + 2)
    late = pltpu.make_async_copy(rest, out_hbm.at[start:], sem.at[1])
    late.start()
    early.wait()
    late.wait()


def kernel(
    n, leads, owner_hbm, hours_hbm, f_hbm, c_hbm, w1_hbm, w2_hbm, wi_hbm, wm_hbm, wo_hbm, o_ref, f_ref, ys, ws, mixed,
    c_ref, w1_ref, w2_ref, wi_ref, wm_ref, wo_ref,
    xs, acc, big_g, gt, wf, wc, wd, wp, proj, prev, foll,
    up_in, down_in, up_out, down_out, owner_ref, hours_ref, small_sem, in_sem,
    up_send, up_recv, down_send, down_recv, lead_send, lead_recv,
):
    height, width, ch = f_ref.shape
    chunks = height // ROWS
    slices = height // SLICE
    half = ROWS // 2
    cells = ROWS * width
    part = c_ref.shape[3]
    ctx_ch = HALVES * part // width
    pieces = HALVES * slices
    per = ch // ctx_ch
    groups = width // per
    temporal = wi_ref.shape[0]
    packs = ch // temporal
    packed_rows = height * width // packs

    def fetch(i):
        source, target = (
            (f_hbm, f_ref), (wi_hbm, wi_ref), (w1_hbm, w1_ref), (w2_hbm, w2_ref),
            (wm_hbm, wm_ref), (wo_hbm, wo_ref), (owner_hbm, owner_ref), (hours_hbm, hours_ref),
        )[i]
        return pltpu.make_async_copy(source, target, in_sem.at[i])

    def fetch_context(half):
        return pltpu.make_async_copy(
            c_hbm.at[:, :, half * part : (half + 1) * part], c_ref.at[:, half], small_sem.at[half]
        )

    z = lax.axis_index("patch")
    lead = lax.axis_index("lead")
    first, last = z == 0, z == n - 1
    lead_first, lead_last = lead == 0, lead == leads - 1

    barrier = pltpu.get_barrier_semaphore()


    for cond, axis, index in (
        (jnp.logical_not(first), "patch", z - 1),
        (jnp.logical_not(last), "patch", z + 1),
        (jnp.logical_not(lead_first), "lead", lead - 1),
        (jnp.logical_not(lead_last), "lead", lead + 1),
    ):
        @pl.when(cond)
        def _(axis=axis, index=index):
            pl.semaphore_signal(barrier, inc=1, device_id={axis: index}, device_id_type=MESH)

    neighbours = (
        4
        - first.astype(jnp.int32)
        - last.astype(jnp.int32)
        - lead_first.astype(jnp.int32)
        - lead_last.astype(jnp.int32)
    )
    for i in (6, 7, 0, 1):
        fetch(i).start()
    for half in range(HALVES):
        fetch_context(half).start()
    for i in range(2, 6):
        fetch(i).start()

    pl.semaphore_wait(barrier, neighbours)

    def up_copy(src, c, half):
        at = HALVES * c + half
        return pltpu.make_async_remote_copy(
            src_ref=src, dst_ref=up_in.at[c, half], send_sem=up_send.at[at],
            recv_sem=up_recv.at[at], device_id={"patch": z + 1}, device_id_type=MESH,
        )

    def down_copy(src, c, half):
        at = HALVES * c + half
        return pltpu.make_async_remote_copy(
            src_ref=src, dst_ref=down_in.at[c, half], send_sem=down_send.at[at],
            recv_sem=down_recv.at[at], device_id={"patch": z - 1}, device_id_type=MESH,
        )

    @pl.when(first)
    def _():
        @pl.loop(0, slices)
        def _(c):
            for half in range(HALVES):
                up_copy(c_hbm.at[c, :, half * part : (half + 1) * part], c, half).start()

    @pl.when(last)
    def _():
        @pl.loop(0, slices)
        def _(c):
            for half in range(HALVES):
                down_copy(c_hbm.at[c, :, half * part : (half + 1) * part], c, half).start()

    def project():
        fetch(0).wait()
        fetch(1).wait()
        wp[...] = jnp.zeros_like(wp)
        parts = []
        whole = f_ref[...].reshape(height // packs, packs, width, ch)
        for q in range(packs):
            wp[q * temporal : (q + 1) * temporal, q * ch : (q + 1) * ch] = wi_ref[...]
            parts.append(whole[:, q].reshape(packed_rows, ch))
        total = lax.dot_general(
            jnp.concatenate(parts, axis=1), wp[...], (((1,), (1,)), ((), ())),
            preferred_element_type=F32,
        )
        proj[...] = total.astype(BF16)

    def pack_weights(target, source):
        zero = jnp.zeros((ch, ch), BF16)
        for r in range(4):
            for b in range(3):
                at = (3 * r + b) * ch
                for q in range(2):
                    a = r - q
                    block = source[3 * a + b, :ch, :] if 0 <= a <= 2 else zero
                    target[at : at + ch, q * ch : (q + 1) * ch] = block

    def pack_context_weights():
        small = jnp.zeros((ctx_ch, ch), BF16)
        for a in range(3):
            taps = [w1_ref[3 * a + b, ch:, :] for b in range(3)]
            for i, pair in enumerate(
                ((taps[1], taps[0]), (taps[2], taps[1]), (taps[0], small), (small, taps[2]))
            ):
                at = a * 4 * ctx_ch + i * ctx_ch
                for q in range(2):
                    wc[at : at + ctx_ch, q * ch : (q + 1) * ch] = pair[q]

    def pack_lead_weights():
        wd[...] = jnp.zeros_like(wd)
        ws[12 * ch :] = jnp.zeros((packs // 2 * ch, 2 * ch), BF16)
        for q in range(packs):
            at = slice(q * temporal, (q + 1) * temporal)
            for t in range(3):
                wd[t, at, at] = wm_ref[t]
            low = (12 + q // 2) * ch + q * temporal
            ws[low : low + temporal, q % 2 * ch : (q % 2 + 1) * ch] = wo_ref[...]

    def put_shifted(target, v, row, count):
        size = count * width
        col = lax.rem(lax.broadcasted_iota(jnp.int32, (size, ch), 0), width)
        left = jnp.where(col == 0, 0.0, pltpu.roll(v, 1, 0))
        right = jnp.where(col == width - 1, 0.0, pltpu.roll(v, size - 1, 0))
        for b, value in enumerate((left, v, right)):
            target[b, pl.ds(1 + row, count)] = value.astype(BF16).reshape(count, width, ch)

    def clear_edges():
        edge = jnp.zeros((width, ch), BF16)
        for target in (xs, ys):
            for b in range(3):
                target[b, 0] = edge
                target[b, height + 1] = edge
        big_g[0] = jnp.zeros(big_g.shape[1:], BF16)
        big_g[height + 1] = jnp.zeros(big_g.shape[1:], BF16)

    def shift_features():
        @pl.loop(0, chunks)
        def _(k):
            put_shifted(xs, f_ref[pl.ds(k * ROWS, ROWS)].reshape(cells, ch).astype(F32), k * ROWS, ROWS)

    def lead_copy(side):
        landing, index = ((prev, lead + 1), (foll, lead - 1))[side]
        return pltpu.make_async_remote_copy(
            src_ref=proj, dst_ref=landing, send_sem=lead_send.at[side],
            recv_sem=lead_recv.at[side], device_id={"lead": index}, device_id_type=MESH,
        )

    def send_projection():
        @pl.when(jnp.logical_not(lead_last))
        def _():
            lead_copy(0).start()

        @pl.when(jnp.logical_not(lead_first))
        def _():
            lead_copy(1).start()

    def feature_conv(k):
        out = split_pairs(conv_pairs(xs, wf, k * ROWS, ROWS), ROWS, width)
        acc[pl.ds(k * ROWS, ROWS)] = jnp.stack(out, axis=1).reshape(ROWS, width, ch)

    def mix_wait():
        @pl.when(jnp.logical_not(lead_first))
        def _():
            lead_copy(0).wait_recv()

        @pl.when(jnp.logical_not(lead_last))
        def _():
            lead_copy(1).wait_recv()

        @pl.when(lead_first)
        def _():
            prev[...] = jnp.zeros_like(prev)

        @pl.when(lead_last)
        def _():
            foll[...] = jnp.zeros_like(foll)

    def mix(i):
        now = hours_ref[lead]
        before = hours_ref[jnp.maximum(lead - 1, 0)]
        after = hours_ref[jnp.minimum(lead + 1, leads - 1)]

        def gain(later, earlier, absent):
            gap = jnp.full((1, ch), (later - earlier).astype(F32), F32)
            return jnp.where(absent, 0.0, jnp.exp(-0.5 * (gap - 1.0)))

        gain_prev = gain(now, before, lead_first)
        gain_next = gain(after, now, lead_last)
        size = packed_rows // PARTS
        rows = pl.ds(pl.multiple_of(i * size, size), size)
        value = gain_prev * dot(prev[rows], wd[0])
        value = value + dot(proj[rows], wd[1])
        value = value + gain_next * dot(foll[rows], wd[2])
        mixed[rows] = value.astype(BF16)

    total_rows = SLICE * groups

    def take_context(k):
        lane = lax.broadcasted_iota(jnp.int32, (total_rows, ch), 1)
        group = lax.rem(lax.broadcasted_iota(jnp.int32, (total_rows, ch), 0), groups)
        owner = owner_ref[lead]
        per_half = groups // HALVES
        for half in range(HALVES):
            low = jnp.where(owner < z, up_in[k, half], down_in[k, half])
            g = jnp.where(owner == z, c_ref[k, half], low).astype(F32)
            for j in range(per_half):
                at = half * per_half + j
                gt[pl.ds(at, SLICE, stride=groups), :] = g[:, j * ch : (j + 1) * ch]
        x = gt[...]
        y = pltpu.roll(x, ctx_ch, 1)
        back = jnp.where(group == 0, 0.0, pltpu.roll(y, 1, 0))
        ahead = jnp.where(group == groups - 1, 0.0, pltpu.roll(y, total_rows - 1, 0))
        beside = jnp.where(lane < ctx_ch, back, ahead)
        rows = pl.ds(1 + k * SLICE, SLICE)
        big_g[rows, :, :ch] = x.astype(BF16).reshape(SLICE, groups, ch)
        big_g[rows, :, ch:] = beside.astype(BF16).reshape(SLICE, groups, ch)

    def activate(row, count):
        size = count * groups
        lhs = [big_g[pl.ds(row + a, count)].reshape(size, 2 * ch) for a in range(3)]
        out = dot(jnp.concatenate(lhs, axis=1), wc[...])
        v = silu(out.reshape(2 * size, ch) + acc[pl.ds(row, count)].reshape(2 * size, ch))
        put_shifted(ys, v, row, count)

    def finish(row, count):
        o_ref[pl.ds(row, count)] = finished(f_ref, ys, ws, mixed, row, count)

    project()
    send_projection()
    shift_features()
    clear_edges()
    fetch(2).wait()
    pack_weights(wf, w1_ref)
    pack_context_weights()

    @pl.loop(0, EARLY)
    def _(k):
        feature_conv(k)

    for half in range(HALVES):
        fetch_context(half).wait()
    fetch(6).wait()
    fetch(7).wait()

    def pack_rest():
        for i in (3, 4, 5):
            fetch(i).wait()
        pack_weights(ws, w2_ref)
        pack_lead_weights()

    def wait_piece(copy, landed, c):
        for half in range(HALVES):
            copy(landed.at[c, half], c, half).wait_recv()

    edge = first | last

    @pl.when(edge)
    def _():
        @pl.loop(EARLY, chunks)
        def _(k):
            feature_conv(k)

        pack_rest()
        mix_wait()

        @pl.loop(0, PARTS)
        def _(i):
            mix(i)


        def receive(c):
            @pl.when(first)
            def _():
                wait_piece(down_copy, down_in, c)

            @pl.when(last)
            def _():
                wait_piece(up_copy, up_in, c)

            take_context(c)

        @pl.loop(0, slices)
        def _(c):
            receive(c)

            @pl.when(c == 1)
            def _():
                activate(0, ROWS - 1)
                finish(0, ROWS - 2)

            @pl.when((c > 1) & (c < slices - 2) & (lax.rem(c, 2) == 1))
            def _():
                row = lax.div(c, 2) * ROWS
                activate(row - 1, ROWS)
                finish(row - 2, ROWS)


    @pl.when(jnp.logical_not(edge))
    def _():
        up_at, down_at = LAG * z, LAG * (n - 1 - z)
        ready_at = jnp.maximum(up_at, down_at)
        up_first = up_at >= down_at
        start_at = jnp.minimum(up_at, down_at)
        owner = owner_ref[lead]
        mine = owner == z

        def go(at, copy, landed, out):
            c, half = lax.div(at, HALVES), lax.rem(at, HALVES)

            @pl.when((at >= 0) & (at < pieces))
            def _():
                copy(landed.at[c, half], c, half).wait_recv()
                out[c, half] = jnp.where(mine, c_ref[c, half], landed[c, half])
                copy(out.at[c, half], c, half).start()

        @pl.loop(start_at, ready_at + pieces + LATE)
        def _(s):
            @pl.when(up_first)
            def _():
                go(s - up_at, up_copy, up_in, up_out)
                go(s - down_at, down_copy, down_in, down_out)

            @pl.when(jnp.logical_not(up_first))
            def _():
                go(s - down_at, down_copy, down_in, down_out)
                go(s - up_at, up_copy, up_in, up_out)

            t = s - start_at

            mix_at = chunks - EARLY + 1

            @pl.when(t < mix_at + PARTS)
            def _():
                @pl.when(t < chunks - EARLY)
                def _():
                    feature_conv(t + EARLY)

                @pl.when(t == chunks - EARLY)
                def _():
                    pack_rest()

                @pl.when(t == mix_at)
                def _():
                    mix_wait()

                @pl.when(t >= mix_at)
                def _():
                    mix(t - mix_at)

            r = s - ready_at - LATE

            @pl.when(r >= 0)
            def _():
                take_context(r)

                @pl.when(r == 1)
                def _():
                    activate(0, ROWS - 1)

                @pl.when(r == 2)
                def _():
                    finish(0, ROWS - 2)

                odd = lax.rem(r, 2)
                row = (r - odd) * SLICE

                @pl.when((r > 2) & (r < slices - 2) & (odd == 1))
                def _():
                    activate(row - 1, ROWS)

                @pl.when((r > 2) & (odd == 0))
                def _():
                    finish(row - ROWS - 2, ROWS)

    activate(height - ROWS - 1, ROWS + 1)

    @pl.loop(0, slices)
    def _(c):
        for half in range(HALVES):
            @pl.when(jnp.logical_not(last))
            def _():
                up_copy(c_ref.at[c, half], c, half).wait_send()

            @pl.when(jnp.logical_not(first))
            def _():
                down_copy(c_ref.at[c, half], c, half).wait_send()

    @pl.when(jnp.logical_not(lead_last))
    def _():
        lead_copy(0).wait_send()

    @pl.when(jnp.logical_not(lead_first))
    def _():
        lead_copy(1).wait_send()


def per_device(
    features, context, owner, hours, w_first, w_second, w_lead_in, w_lead_mix, w_lead_out
):
    n, leads = lax.axis_size("patch"), lax.axis_size("lead")
    _, _, height, width, ch = features.shape
    temporal = w_lead_in.shape[1]
    merged = context.shape[3]
    cells = ROWS * width
    groups = merged // ch
    packs = ch // temporal
    packed_rows = height * width // packs
    vmem = pltpu.VMEM
    slices = height // SLICE
    pieces = HALVES * slices
    line = vmem((slices, HALVES, SLICE, merged // HALVES), BF16)
    hbm = pl.BlockSpec(memory_space=pl.ANY)
    dma = pltpu.SemaphoreType.DMA
    held = [
        vmem((height, width, ch), BF16),
        vmem((height, width, ch), BF16),
        vmem((3, height + 2, width, ch), BF16),
        vmem(((12 + packs // 2) * ch, 2 * ch), BF16),
        vmem((packed_rows, ch), BF16),
    ]
    most = pl.pallas_call(
        functools.partial(kernel, n, leads),
        out_shape=held,
        in_specs=[hbm] * 9,
        out_specs=[pl.BlockSpec(memory_space=pltpu.VMEM)] * len(held),
        scratch_shapes=[
            line,
            vmem(w_first.shape, BF16),
            vmem(w_second.shape, BF16),
            vmem((temporal, ch), BF16),
            vmem(w_lead_mix.shape, BF16),
            vmem(w_lead_out.shape, BF16),
            vmem((3, height + 2, width, ch), BF16),
            vmem((height, width, ch), F32),
            vmem((height + 2, groups, 2 * ch), BF16),
            vmem((SLICE * groups, ch), F32),
            vmem((12 * ch, 2 * ch), BF16),
            vmem((6 * ch, 2 * ch), BF16),
            vmem((3, ch, ch), BF16),
            vmem((ch, packs * ch), BF16),
            vmem((packed_rows, ch), BF16),
            vmem((packed_rows, ch), BF16),
            vmem((packed_rows, ch), BF16),
            line, line, line, line,
            pltpu.SMEM(owner.shape, jnp.int32), pltpu.SMEM(hours.shape, jnp.int32),
            dma((HALVES,)), dma((8,)),
            dma((pieces,)), dma((pieces,)), dma((pieces,)), dma((pieces,)), dma((2,)), dma((2,)),
        ],
        compiler_params=pltpu.CompilerParams(
            collective_id=0, has_side_effects=True, vmem_limit_bytes=LIMIT
        ),
    )(
        owner, hours, features[0, 0], context.reshape(slices, SLICE, merged),
        w_first, w_second, w_lead_in.T, w_lead_mix, w_lead_out,
    )
    out = pl.pallas_call(
        last_rows,
        out_shape=jax.ShapeDtypeStruct((height, width, ch), BF16),
        in_specs=[pl.BlockSpec(memory_space=pltpu.VMEM)] * len(held),
        out_specs=hbm,
        scratch_shapes=[vmem((ROWS + 2, width, ch), BF16), dma((2,))],
        compiler_params=pltpu.CompilerParams(vmem_limit_bytes=16 * 2**20),
    )(*most)
    return out[None, None]


def solution(mesh):
    placed = (
        P(("grp", "lead"), "patch", None, None, None),
        P("patch", ("grp", "lead"), None, None),
        P("grp"),
        P("grp"),
        P(),
        P(),
        P(),
        P(),
        P(),
    )
    return jax.shard_map(
        per_device,
        mesh=mesh,
        in_specs=placed,
        out_specs=P(("grp", "lead"), "patch", None, None, None),
        check_vma=False,
    )
```
